32 devices in a mesh: table: 2 (over x), batch: 16 (over z, y, core).
Axes of the slice: x: 2, y: 2, z: 4, core: 2. Of those that a mesh axis runs over, the one named last changes fastest.
Arguments:
- x_first: bfloat16 [2048, 4096], P('batch', 'table'), may hold values from -6 to 6
- x_layer: bfloat16 [2048, 4096], P('batch', 'table'), may hold values from -6 to 6
- pre_act: bfloat16 [2048, 4096], P('batch', 'table'), may hold values from -8 to 8
- gamma: float32 [4096], P('table'), may hold values from 0.3 to 3
- weight: float32 [4096, 4096], P('table', 'batch'), may hold values from -0.09375 to 0.09375
- cotangent: bfloat16 [2048, 4096], P('batch', 'table'), may hold values from -12 to 12
Outputs:
- grad_first: bfloat16 [2048, 4096], P('batch', 'table')
- grad_layer: bfloat16 [2048, 4096], P('batch', 'table')
- grad_weight: float32 [4096, 4096], P('table', 'batch')
- grad_bias: float32 [4096], P('table')
- grad_gamma: float32 [4096], P('table')
The draws below stay inside these ranges and needn't reach their ends.
All inputs are finite; a program needn't handle non-finite values.
Results may differ from the reference program's by a relative error of at most 0.005.
Values may be sent and summed in bfloat16 or wider, within the bound.
A program may use at most 128 MiB of HBM per device.

```python
import math
import jax
import jax.numpy as jnp
from jax import lax

D = 4096
SAMPLES = 2048


def draw_cotangent(key, part):
    key_one = jax.random.fold_in(key, 11)
    row_scale = 1.0 + 2.0 * jnp.arange(SAMPLES, dtype=jnp.float32) / SAMPLES
    base = jnp.clip(jax.random.normal(key_one, (SAMPLES, D), jnp.float32), -4.0, 4.0)
    values = base * row_scale[:, None]
    return values.astype(jnp.bfloat16)


def block_levels(key, extent, pieces, least, largest):
    factor_of = 1.0
    for position, parts in pieces:
        draws = jax.random.uniform(jax.random.fold_in(jax.random.fold_in(key, 6), position), (parts,), jnp.float32, least / len(pieces), largest / len(pieces))
        factor_of = factor_of * jnp.repeat(jnp.exp(draws), extent[position] // parts).reshape((-1,) + (1,) * (len(extent) - 1 - position))
    return factor_of


def scatter_about(rng, dims, width, limit, split=(), kind=jnp.bfloat16):
    array = width * jax.random.normal(rng, dims, jnp.float32)
    if split:
        array = array * block_levels(rng, dims, split, -0.22, 0.18)
    return jnp.clip(array, -limit, limit).astype(kind)


def setup_inputs(seed: int = 0) -> dict:
    streams_of = jax.random.split(jax.random.key(seed), 7)
    x_first = scatter_about(streams_of[0], (SAMPLES, D), 1.0, 6.0, ((0, 16), (1, 2)))
    x_layer = scatter_about(streams_of[1], (SAMPLES, D), 1.0, 6.0, ((0, 16), (1, 2)))
    pre_act = scatter_about(streams_of[2], (SAMPLES, D), 1.5, 8.0, ((0, 16), (1, 2)))
    gamma = jnp.clip(jnp.exp(math.log(3.0) - 2.3025851 * jax.random.uniform(streams_of[3], (D,), jnp.float32) ** block_levels(streams_of[3], (D,), ((0, 2),), -0.2, 0.2)), 0.3, 3.0)
    weight = scatter_about(streams_of[4], (D, D), D ** -0.5, 0.09375, ((0, 2), (1, 16)), jnp.float32)
    cotangent = draw_cotangent(jax.random.fold_in(streams_of[6], 71), 0)
    return {"x_first": x_first, "x_layer": x_layer, "pre_act": pre_act, "gamma": gamma, "weight": weight, "cotangent": cotangent}


def reference(x_first, x_layer, pre_act, gamma, weight, cotangent):
    weight_bf = weight.astype(jnp.bfloat16)
    pre_full = pre_act.astype(jnp.float32)
    gate_tanh = jnp.tanh(gamma[None, :] * pre_full)
    hidden = pre_full * gate_tanh
    cot_full = cotangent.astype(jnp.float32)
    grad_hidden = cot_full * x_first.astype(jnp.float32)
    grad_first = (cot_full * hidden).astype(jnp.bfloat16)
    slope = 1.0 - gate_tanh * gate_tanh
    grad_pre = (grad_hidden * (gate_tanh + gamma[None, :] * pre_full * slope)).astype(jnp.bfloat16)
    grad_gamma = jnp.sum(grad_hidden * pre_full * pre_full * slope, axis=0)
    grad_bias = jnp.sum(grad_pre.astype(jnp.float32), axis=0)
    grad_weight = lax.dot_general(grad_pre, x_layer, (((0,), (0,)), ((), ())), preferred_element_type=jnp.float32)
    grad_layer = (cot_full + jnp.dot(grad_pre, weight_bf, preferred_element_type=jnp.float32)).astype(jnp.bfloat16)
    return grad_first, grad_layer, grad_weight, grad_bias, grad_gamma
```

```python
import functools

import jax
import jax.numpy as jnp
from jax import lax
from jax.experimental import pallas as pl
from jax.experimental.pallas import tpu as pltpu
from jax.sharding import PartitionSpec as P

MESH = pl.DeviceIdType.MESH
F32 = jnp.float32
BF16 = jnp.bfloat16


def exchange(
    nb, phases, parts,
    x_ref, act_ref, cot_ref, gamma_ref, cols_ref, weight_ref,
    wsum_ref, ret_ref, total_ref,
    held, xall, mine, theirs, inbox, summed, layover, guest, small_ref, smalls, half_ref, away_ref,
    wfull, wbf, wsend, winbox,
    line_send, line_recv, sib_send, sib_recv, own_sem, w_sem, x_send, x_on, x_recv, swap,
    pair_send, pair_recv, sum_send, lay_recv, lay_send, ret_recv, small_send, small_recv, away_sem,
    share_send, share_recv, load_sem,
):
    rows, outs = x_ref.shape
    cols = wfull.shape[1]
    nz, per = nb // 4, nb // 2
    hz, last = nz // 2, nz - 1
    chunks = phases * parts
    wide = outs // chunks
    t, b = lax.axis_index("table"), lax.axis_index("batch")
    z, y, c = b // 4, (b // 2) % 2, b % 2
    other = 1 - t
    home = z // hz

    def device(zz, yy, cc):
        return (zz * 2 + yy) * 2 + cc

    def column(zz, yy, cc):
        return ((zz % hz) * 2 + yy) * 2 + cc

    sibling, across = device(z, y, 1 - c), device(z, 1 - y, c)
    came = (z, last - z)
    goes = (z < last, z > 0)
    ahead = (b + 4, b - 4)

    def origin(d, k):
        return z - 1 - k if d == 0 else z + 1 + k

    def core_rows(core):
        return pl.ds(pl.multiple_of(core * rows, rows), rows)

    def piece(zz, core, chunk):
        return held.at[zz, core_rows(core), pl.ds(chunk * wide, wide)]

    def xblock(yy, zz, core):
        return xall.at[yy, zz, core_rows(core), :]

    def features(ref, j):
        return ref.at[j] if len(ref.shape) == 3 else ref.at[:, pl.ds(pl.multiple_of(j * cols, cols), cols)]

    def done(ref, sem):
        pltpu.make_async_copy(ref, ref, sem).wait()

    def send(src, dst, ssem, rsem, tt, bb):
        return pltpu.make_async_remote_copy(
            src_ref=src, dst_ref=dst, send_sem=ssem, recv_sem=rsem, device_id=(tt, bb), device_id_type=MESH
        ).start()

    def each(k, act):
        for d in range(2):
            @pl.when(k < came[d])
            def _():
                act(origin(d, k))

    load_w = pltpu.make_async_copy(weight_ref, wfull, load_sem)
    load_w.start()
    barrier = pltpu.get_barrier_semaphore()

    def greet(tt, bb):
        pl.semaphore_signal(barrier, inc=1, device_id=(tt, bb), device_id_type=MESH)

    greet(other, b)
    greet(t, across)

    def along(act):
        def step(i, carry):
            bb = device(i // 2, y, i % 2)

            @pl.when(bb != b)
            def _():
                act(i, bb)

            return carry

        lax.fori_loop(0, 2 * nz, step, 0)

    along(lambda i, bb: greet(t, bb))
    small_ref[...] = jnp.zeros_like(small_ref)
    tall = 16 if rows % 16 == 0 else rows
    lanes = 512 if outs % 512 == 0 else outs

    def gate(i, carry):
        at = pl.ds(pl.multiple_of(i * tall, tall), tall)
        put = pl.ds(pl.multiple_of(c * rows + i * tall, tall), tall)
        for lane in range(0, outs, lanes):
            to = pl.ds(lane, lanes)
            sharp = gamma_ref[:, to]
            act = act_ref[at, to].astype(F32)
            tanh = jnp.tanh(sharp * act)
            hidden = cot_ref[at, to].astype(F32) * x_ref[at, to].astype(F32)
            slope = 1.0 - tanh * tanh
            pre = (hidden * (tanh + sharp * act * slope)).astype(BF16)
            held[z, put, to] = pre
            small_ref[0:1, to] += jnp.sum(pre.astype(F32), axis=0, keepdims=True)
            small_ref[1:2, to] += jnp.sum(hidden * act * act * slope, axis=0, keepdims=True)
        return carry

    lax.fori_loop(0, rows // tall, gate, 0)
    load_w.wait()
    wbf[y] = wfull[...].astype(BF16)
    pl.semaphore_wait(barrier, 2 * nz + 1)

    def give_own(d, phase):
        @pl.when(goes[d])
        def _():
            for chunk in range(phase * parts, phase * parts + parts):
                here = piece(z, c, chunk)
                send(here, here, line_send.at[d, 0, chunk], line_recv.at[d, 0, chunk], t, ahead[d])

    give_own(0, 0)
    give_own(1, 0)
    own_rows = held.at[z, core_rows(c), :]
    send(own_rows, own_rows, own_sem.at[0], own_sem.at[1], t, sibling)
    send(wbf.at[y], wbf.at[y], w_sem.at[0], w_sem.at[1], t, across)

    odd = c == 1
    side = jnp.where(odd, other, t)

    def target(j):
        return device(side * hz + j // 4, y, j % 2)

    def give_columns(source):
        def give(i, carry):
            j = (i + column(z, 0, c)) % per
            bb = target(j)
            there = xblock((j // 2) % 2, z, c)
            rsem = x_recv.at[(j // 2) % 2, z, c]

            @pl.when(bb == b)
            def _():
                pltpu.make_async_copy(features(source, j), there, rsem).start()

            @pl.when(bb != b)
            def _():
                send(features(source, j), there, x_send.at[j], rsem, t, bb)

            return carry

        lax.fori_loop(0, per, give, 0)

    @pl.when(odd)
    def _():
        send(cols_ref, guest, swap.at[0], swap.at[1], other, b)

    @pl.when(jnp.logical_not(odd))
    def _():
        give_columns(cols_ref)

    along(lambda i, bb: send(small_ref, smalls.at[2 * z + c], small_send.at[i], small_recv.at[2 * z + c], t, bb))
    smalls[2 * z + c] = small_ref[...]
    lands = (home + t) % 2

    def pass_columns(zz):
        for yy in range(2):
            ref = xblock(yy, zz, lands)
            done(ref, x_recv.at[yy, zz, lands])
            send(ref, ref, x_on.at[yy, zz], x_recv.at[yy, zz, lands], other, b)

    def take_columns():
        def step(zz, carry):
            for yy in range(2):
                done(xblock(yy, zz, 1 - lands), x_recv.at[yy, zz, 1 - lands])
            return carry

        lax.fori_loop(0, nz, step, 0)

    def half(zz, which, yy):
        return jnp.dot(held[zz, core_rows(which), :], wbf[yy], preferred_element_type=F32)

    def multiply(zz):
        for yy in range(2):
            theirs[zz, yy] = half(zz, other, yy).astype(BF16)
        send(theirs.at[zz], inbox.at[zz], pair_send.at[zz], pair_recv.at[zz], other, b)
        for yy in range(2):
            mine[zz, yy] = half(zz, t, yy)

    def give_sum(zz):
        done(inbox.at[zz], pair_recv.at[zz])
        summed[zz] = (mine[zz] + inbox[zz].astype(F32)).astype(BF16)
        bb = device(zz, y, t)
        for yy in range(2):
            slot = column(z, yy, c)
            for stays, dst, rsem in ((True, ret_ref, ret_recv), (False, layover, lay_recv)):
                right = (home == t) if stays else (home != t)

                @pl.when(jnp.logical_and(right, bb == b))
                def _():
                    pltpu.make_async_copy(summed.at[zz, yy], features(dst, slot), rsem.at[slot]).start()

                @pl.when(jnp.logical_and(right, bb != b))
                def _():
                    send(summed.at[zz, yy], features(dst, slot), sum_send.at[zz, yy], rsem.at[slot], t, bb)

    def pass_sum(zz):
        @pl.when(jnp.logical_and(c == t, zz // hz != t))
        def _():
            for yy in range(2):
                for cc in range(2):
                    j = column(zz, yy, cc)
                    done(layover.at[j], lay_recv.at[j])
                    send(layover.at[j], features(ret_ref, j), lay_send.at[j], ret_recv.at[j], other, b)

    group = 4 if nz % 4 == 0 else nz

    def product(chunk, yy):
        to = pl.ds(chunk * wide, wide)
        total = None
        for g in range(0, nz, group):
            zs = pl.ds(g, group)
            term = lax.dot_general(
                held[zs, :, to].reshape(group * 2 * rows, wide),
                xall[yy, zs].reshape(group * 2 * rows, cols),
                (((0,), (0,)), ((), ())),
                preferred_element_type=F32,
            )
            total = term if total is None else total + term
        return total

    def give_share(chunk):
        wsend[chunk] = product(chunk, 1 - y).astype(BF16)
        send(wsend.at[chunk], winbox.at[chunk], share_send.at[chunk], share_recv.at[chunk], t, across)

    def keep_share(chunk):
        wsum_ref[pl.ds(chunk * wide, wide), :] = product(chunk, y)

    def hop(phase, k):
        for chunk in range(phase * parts, phase * parts + parts):
            for d in range(2):
                @pl.when(k < came[d])
                def _():
                    here = piece(origin(d, k), c, chunk)
                    done(here, line_recv.at[d, k, chunk])

                    @pl.when(goes[d])
                    def _():
                        send(here, here, line_send.at[d, k + 1, chunk], line_recv.at[d, k + 1, chunk], t, ahead[d])

                    send(here, here, sib_send.at[d, k, chunk], sib_recv.at[d, k, chunk], t, sibling)

        if phase + 1 < phases:
            for d in range(2):
                @pl.when(k == came[d])
                def _():
                    give_own(d, phase + 1)

    def meet(phase, k):
        for d in range(2):
            @pl.when(k < came[d])
            def _():
                for chunk in range(phase * parts, phase * parts + parts):
                    done(piece(origin(d, k), 1 - c, chunk), sib_recv.at[d, k, chunk])

    for phase in range(phases - 1):
        def gather(k, carry):
            hop(phase, k)
            if phase == 0:
                @pl.when(k == 0)
                def _():
                    @pl.when(odd)
                    def _():
                        done(guest, swap.at[1])
                        give_columns(guest)

                    pass_columns(z)

                each(k, pass_columns)
            meet(phase, k)
            return carry

        lax.fori_loop(0, last, gather, 0)
    along(lambda i, bb: done(smalls.at[i], small_recv.at[i]))
    half_ref[...] = jnp.sum(smalls[...], axis=0)
    send(half_ref, away_ref, away_sem.at[0], away_sem.at[1], t, across)
    theirs_rows = held.at[z, core_rows(1 - c), :]
    done(theirs_rows, own_sem.at[1])
    done(wbf.at[1 - y], w_sem.at[1])
    multiply(z)

    early = chunks - parts

    def finish(k, carry):
        hop(phases - 1, k)
        meet(phases - 1, k)
        each(k, multiply)

        @pl.when(k == 0)
        def _():
            give_sum(z)
            take_columns()

        @pl.when(k > 0)
        def _():
            each(k - 1, give_sum)

        @pl.when(k == 1)
        def _():
            pass_sum(z)

        @pl.when(k > 1)
        def _():
            each(k - 2, pass_sum)

        for chunk in range(early):
            @pl.when(k == min(chunk, last - 1))
            def _():
                give_share(chunk)
                keep_share(chunk)

        return carry

    lax.fori_loop(0, last, finish, 0)
    for chunk in range(early, chunks):
        give_share(chunk)
    each(last - 1, give_sum)
    if last == 1:
        pass_sum(z)
    else:
        each(last - 2, pass_sum)
    for chunk in range(early, chunks):
        keep_share(chunk)
    each(last - 1, pass_sum)
    for chunk in range(chunks):
        done(winbox.at[chunk], share_recv.at[chunk])
        wsum_ref[pl.ds(chunk * wide, wide), :] += winbox[chunk].astype(F32)
    done(away_ref, away_sem.at[1])
    total_ref[...] = half_ref[...] + away_ref[...]

    along(lambda i, bb: done(small_ref, small_send.at[i]))
    done(half_ref, away_sem.at[0])
    done(own_rows, own_sem.at[0])
    done(wbf.at[y], w_sem.at[0])
    for chunk in range(chunks):
        done(wsend.at[chunk], share_send.at[chunk])

    @pl.when(odd)
    def _():
        done(cols_ref, swap.at[0])

    def sent_columns(j, carry):
        @pl.when(target(j) != b)
        def _():
            done(features(cols_ref, j), x_send.at[j])

        return carry

    lax.fori_loop(0, per, sent_columns, 0)

    def sent_line(zz, carry):
        for yy in range(2):
            done(xblock(yy, zz, lands), x_on.at[yy, zz])

            @pl.when(device(zz, y, t) != b)
            def _():
                done(summed.at[zz, yy], sum_send.at[zz, yy])

        done(theirs.at[zz], pair_send.at[zz])
        return carry

    lax.fori_loop(0, nz, sent_line, 0)

    def back(j, carry):
        done(features(ret_ref, j), ret_recv.at[j])

        @pl.when(c == t)
        def _():
            done(layover.at[j], lay_send.at[j])

        return carry

    lax.fori_loop(0, per, back, 0)

    def sent_pieces(k, carry):
        for chunk in range(chunks):
            for d in range(2):
                @pl.when(jnp.logical_and(goes[d], k <= came[d]))
                def _():
                    done(piece(z, c, chunk), line_send.at[d, k, chunk])

                @pl.when(k < came[d])
                def _():
                    done(piece(z, c, chunk), sib_send.at[d, k, chunk])

        return carry

    lax.fori_loop(0, last, sent_pieces, 0)


def run_exchange(nb, x_first, pre_act, cotangent, gamma, columns, weight):
    rows, outs = x_first.shape
    cols = weight.shape[1]
    nz, per = nb // 4, nb // 2
    last = nz - 1
    phases, parts = 2, 2
    chunks = phases * parts
    wide = outs // chunks
    dma = pltpu.SemaphoreType.DMA
    vmem = pl.BlockSpec(memory_space=pltpu.VMEM)
    return pl.pallas_call(
        functools.partial(exchange, nb, phases, parts),
        out_shape=(
            jax.ShapeDtypeStruct((outs, cols), F32),
            jax.ShapeDtypeStruct(columns.shape, BF16),
            jax.ShapeDtypeStruct((2, outs), F32),
        ),
        in_specs=[vmem] * 5 + [pl.BlockSpec(memory_space=pl.ANY)],
        out_specs=(vmem,) * 3,
        scratch_shapes=[
            pltpu.VMEM((nz, 2 * rows, outs), BF16),
            pltpu.VMEM((2, nz, 2 * rows, cols), BF16),
            pltpu.VMEM((nz, 2, rows, cols), F32),
            pltpu.VMEM((nz, 2, rows, cols), BF16),
            pltpu.VMEM((nz, 2, rows, cols), BF16),
            pltpu.VMEM((nz, 2, rows, cols), BF16),
            pltpu.VMEM((per, rows, cols), BF16),
            pltpu.VMEM(columns.shape, BF16),
            pltpu.VMEM((2, outs), F32),
            pltpu.VMEM((2 * nz, 2, outs), F32),
            pltpu.VMEM((2, outs), F32),
            pltpu.VMEM((2, outs), F32),
            pltpu.VMEM((outs, cols), F32),
            pltpu.VMEM((2, outs, cols), BF16),
            pltpu.VMEM((chunks, wide, cols), BF16),
            pltpu.VMEM((chunks, wide, cols), BF16),
            dma((2, last, chunks)),
            dma((2, last, chunks)),
            dma((2, last, chunks)),
            dma((2, last, chunks)),
            dma((2,)),
            dma((2,)),
            dma((per,)),
            dma((2, nz)),
            dma((2, nz, 2)),
            dma((2,)),
            dma((nz,)),
            dma((nz,)),
            dma((nz, 2)),
            dma((per,)),
            dma((per,)),
            dma((per,)),
            dma((2 * nz,)),
            dma((2 * nz,)),
            dma((2,)),
            dma((chunks,)),
            dma((chunks,)),
            dma,
        ],
        compiler_params=pltpu.CompilerParams(
            collective_id=0, has_side_effects=True, vmem_limit_bytes=60 * 1024 * 1024
        ),
    )(x_first, pre_act, cotangent, gamma, columns, weight)


def results(act_ref, cot_ref, gamma_ref, share_ref, wsum_ref, total_ref, first_ref, layer_ref, weight_ref, bias_ref, sharp_ref):
    act = act_ref[...].astype(F32)
    cot = cot_ref[...].astype(F32)
    first_ref[...] = (cot * (act * jnp.tanh(gamma_ref[...] * act))).astype(BF16)
    layer_ref[...] = (cot + share_ref[...].astype(F32)).astype(BF16)
    weight_ref[...] = wsum_ref[...]
    bias_ref[...] = total_ref[0:1, :]
    sharp_ref[...] = total_ref[1:2, :]


def write_results(pre_act, cotangent, gamma, share, wsum, total):
    rows, outs = pre_act.shape
    cols = wsum.shape[1]
    steps = 4 if rows % 64 == 0 and outs % 32 == 0 else 1
    some = pl.BlockSpec((rows // steps, outs), lambda i: (i, 0))
    tile = pl.BlockSpec((outs // steps, cols), lambda i: (i, 0))
    whole = lambda n: pl.BlockSpec((n, outs), lambda i: (0, 0))
    wide = jax.ShapeDtypeStruct((rows, outs), BF16)
    flat = jax.ShapeDtypeStruct((1, outs), F32)
    return pl.pallas_call(
        results,
        grid=(steps,),
        out_shape=(wide, wide, jax.ShapeDtypeStruct((outs, cols), F32), flat, flat),
        in_specs=[some, some, whole(1), some, tile, whole(2)],
        out_specs=(some, some, tile, whole(1), whole(1)),
    )(pre_act, cotangent, gamma, share, wsum, total)


def shards(nb, x_first, x_layer, pre_act, gamma, weight, cotangent):
    rows = x_layer.shape[0]
    per, cols = nb // 2, weight.shape[1]
    aligned = cols % 128 == 0
    columns = x_layer if aligned else x_layer.reshape(rows, per, cols).transpose(1, 0, 2)
    wsum, share, total = run_exchange(nb, x_first, pre_act, cotangent, gamma[None], columns, weight)
    if not aligned:
        share = share.transpose(1, 0, 2).reshape(rows, per * cols)
    first, layer, grad_weight, bias, sharp = write_results(pre_act, cotangent, gamma[None], share, wsum, total)
    return (first, layer, grad_weight, bias[0], sharp[0])


def solution(mesh):
    assert mesh.shape["table"] == 2 and mesh.shape["batch"] % 8 == 0
    placed = (
        P("batch", "table"),
        P("batch", "table"),
        P("batch", "table"),
        P("table"),
        P("table", "batch"),
        P("batch", "table"),
    )
    return jax.shard_map(
        functools.partial(shards, mesh.shape["batch"]),
        mesh=mesh,
        in_specs=placed,
        out_specs=(
            P("batch", "table"),
            P("batch", "table"),
            P("table", "batch"),
            P("table"),
            P("table"),
        ),
        check_vma=False,
    )
```

```python
import functools

import jax
import jax.numpy as jnp
from jax import lax
from jax.experimental import pallas as pl
from jax.experimental.pallas import tpu as pltpu
from jax.sharding import PartitionSpec as P

MESH = pl.DeviceIdType.MESH
F32 = jnp.float32
BF16 = jnp.bfloat16


def exchange(
    nb, phases, cuts,
    x_in, act_in, cot_in, gamma_ref, cols_ref, weight_ref,
    wsum_out, ret_ref, total_ref,
    x_ref, act_ref, cot_ref, wsum_ref, held, xall, mine, theirs, inbox, summed, layover, guest, small_ref, smalls, half_ref, away_ref,
    wfull, wbf, wsend, winbox,
    line_send, line_recv, sib_send, sib_recv, own_sem, w_sem, x_send, x_on, x_recv, swap,
    pair_send, pair_recv, sum_send, lay_recv, lay_send, ret_recv, small_send, small_recv, away_sem,
    share_send, share_recv, load_sem, out_sem,
):
    rows, outs = x_ref.shape
    cols = wfull.shape[1]
    nz, per = nb // 4, nb // 2
    hz, last = nz // 2, nz - 1
    chunks = len(cuts) - 1
    wide = [cuts[i + 1] - cuts[i] for i in range(chunks)]
    early, late = phases[0], phases[1]
    t, b = lax.axis_index("table"), lax.axis_index("batch")
    z, y, c = b // 4, (b // 2) % 2, b % 2
    other = 1 - t
    home = z // hz

    def device(zz, yy, cc):
        return (zz * 2 + yy) * 2 + cc

    def column(zz, yy, cc):
        return ((zz % hz) * 2 + yy) * 2 + cc

    sibling, across = device(z, y, 1 - c), device(z, 1 - y, c)
    came = (z, last - z)
    goes = (z < last, z > 0)
    ahead = (b + 4, b - 4)

    def origin(d, k):
        return z - 1 - k if d == 0 else z + 1 + k

    def core_rows(core):
        return pl.ds(pl.multiple_of(core * rows, rows), rows)

    def piece(zz, core, chunk):
        return held.at[zz, core_rows(core), pl.ds(cuts[chunk], wide[chunk])]

    def outputs(ref, chunk):
        return ref.at[pl.ds(cuts[chunk], wide[chunk]), :]

    def xblock(yy, zz, core):
        return xall.at[yy, zz, core_rows(core), :]

    def features(ref, j):
        return ref.at[j] if len(ref.shape) == 3 else ref.at[:, pl.ds(pl.multiple_of(j * cols, cols), cols)]

    def done(ref, sem):
        pltpu.make_async_copy(ref, ref, sem).wait()

    def send(src, dst, ssem, rsem, tt, bb):
        return pltpu.make_async_remote_copy(
            src_ref=src, dst_ref=dst, send_sem=ssem, recv_sem=rsem, device_id=(tt, bb), device_id_type=MESH
        ).start()

    def each(k, act):
        for d in range(2):
            @pl.when(k < came[d])
            def _():
                act(origin(d, k))

    barrier = pltpu.get_barrier_semaphore()

    def greet(tt, bb):
        pl.semaphore_signal(barrier, inc=1, device_id=(tt, bb), device_id_type=MESH)

    greet(other, b)
    greet(t, across)

    def along(act):
        def step(i, carry):
            bb = device(i // 2, y, i % 2)

            @pl.when(bb != b)
            def _():
                act(i, bb)

            return carry

        lax.fori_loop(0, 2 * nz, step, 0)

    along(lambda i, bb: greet(t, bb))
    loads = [
        pltpu.make_async_copy(src, dst, load_sem.at[i])
        for i, (src, dst) in enumerate(((act_in, act_ref), (cot_in, cot_ref), (x_in, x_ref), (weight_ref, wfull)))
    ]
    for load in loads:
        load.start()
    small_ref[...] = jnp.zeros_like(small_ref)
    tall = 16 if rows % 16 == 0 else rows
    lanes = 512 if outs % 512 == 0 else outs

    def gate(i, carry):
        at = pl.ds(pl.multiple_of(i * tall, tall), tall)
        put = pl.ds(pl.multiple_of(c * rows + i * tall, tall), tall)
        for lane in range(0, outs, lanes):
            to = pl.ds(lane, lanes)
            sharp = gamma_ref[:, to]
            act = act_ref[at, to].astype(F32)
            tanh = jnp.tanh(sharp * act)
            hidden = cot_ref[at, to].astype(F32) * x_ref[at, to].astype(F32)
            slope = 1.0 - tanh * tanh
            pre = (hidden * (tanh + sharp * act * slope)).astype(BF16)
            held[z, put, to] = pre
            small_ref[0:1, to] += jnp.sum(pre.astype(F32), axis=0, keepdims=True)
            small_ref[1:2, to] += jnp.sum(hidden * act * act * slope, axis=0, keepdims=True)
        return carry

    def give_own(d, phase):
        @pl.when(goes[d])
        def _():
            for chunk in phases[phase]:
                here = piece(z, c, chunk)
                send(here, here, line_send.at[d, 0, chunk], line_recv.at[d, 0, chunk], t, ahead[d])

    odd = c == 1
    side = jnp.where(odd, other, t)

    def target(j):
        return device(side * hz + j // 4, y, j % 2)

    def give_columns(source, chosen):
        def give(j, carry):
            bb = target(j)
            there = xblock((j // 2) % 2, z, c)
            rsem = x_recv.at[(j // 2) % 2, z, c]

            @pl.when(chosen(side * hz + j // 4))
            def _():
                @pl.when(bb == b)
                def _():
                    pltpu.make_async_copy(features(source, j), there, rsem).start()

                @pl.when(bb != b)
                def _():
                    send(features(source, j), there, x_send.at[j], rsem, t, bb)

            return carry

        lax.fori_loop(0, per, give, 0)

    for load in loads[:3]:
        load.wait()
    lax.fori_loop(0, rows // tall, gate, 0)
    loads[3].wait()
    wbf[y] = wfull[...].astype(BF16)
    smalls[2 * z + c] = small_ref[...]
    pl.semaphore_wait(barrier, 2 * nz + 1)
    give_own(0, 0)
    give_own(1, 0)
    own_rows = held.at[z, core_rows(c), :]
    send(own_rows, own_rows, own_sem.at[0], own_sem.at[1], t, sibling)

    @pl.when(odd)
    def _():
        send(cols_ref, guest, swap.at[0], swap.at[1], other, b)

    send(wbf.at[y], wbf.at[y], w_sem.at[0], w_sem.at[1], t, across)
    near = lambda zz: jnp.logical_and(zz <= z + 1, zz >= z - 1)
    beyond = (lambda zz: zz > z + 1, lambda zz: zz < z - 1)

    @pl.when(jnp.logical_not(odd))
    def _():
        give_columns(cols_ref, near)

    along(lambda i, bb: send(small_ref, smalls.at[2 * z + c], small_send.at[i], small_recv.at[2 * z + c], t, bb))
    lands = (home + t) % 2

    def pass_columns(zz):
        for yy in range(2):
            ref = xblock(yy, zz, lands)
            done(ref, x_recv.at[yy, zz, lands])
            send(ref, ref, x_on.at[yy, zz], x_recv.at[yy, zz, lands], other, b)

    def take_columns():
        def step(zz, carry):
            for yy in range(2):
                done(xblock(yy, zz, 1 - lands), x_recv.at[yy, zz, 1 - lands])
            return carry

        lax.fori_loop(0, nz, step, 0)

    def half(zz, which, yy):
        return jnp.dot(held[zz, core_rows(which), :], wbf[yy], preferred_element_type=F32)

    def multiply(zz):
        for yy in range(2):
            theirs[zz, yy] = half(zz, other, yy).astype(BF16)
        send(theirs.at[zz], inbox.at[zz], pair_send.at[zz], pair_recv.at[zz], other, b)
        for yy in range(2):
            mine[zz, yy] = half(zz, t, yy)

    def give_sum(zz):
        done(inbox.at[zz], pair_recv.at[zz])
        summed[zz] = (mine[zz] + inbox[zz].astype(F32)).astype(BF16)
        bb = device(zz, y, t)
        for yy in range(2):
            slot = column(z, yy, c)
            for stays, dst, rsem in ((True, ret_ref, ret_recv), (False, layover, lay_recv)):
                right = (home == t) if stays else (home != t)

                @pl.when(jnp.logical_and(right, bb == b))
                def _():
                    pltpu.make_async_copy(summed.at[zz, yy], features(dst, slot), rsem.at[slot]).start()

                @pl.when(jnp.logical_and(right, bb != b))
                def _():
                    send(summed.at[zz, yy], features(dst, slot), sum_send.at[zz, yy], rsem.at[slot], t, bb)

    def pass_sum(zz):
        @pl.when(jnp.logical_and(c == t, zz // hz != t))
        def _():
            for yy in range(2):
                for cc in range(2):
                    j = column(zz, yy, cc)
                    done(layover.at[j], lay_recv.at[j])
                    send(layover.at[j], features(ret_ref, j), lay_send.at[j], ret_recv.at[j], other, b)

    group = 4 if nz % 4 == 0 else nz

    def product(chunk, yy):
        to = pl.ds(cuts[chunk], wide[chunk])
        total = None
        for g in range(0, nz, group):
            zs = pl.ds(g, group)
            term = lax.dot_general(
                held[zs, :, to].reshape(group * 2 * rows, wide[chunk]),
                xall[yy, zs].reshape(group * 2 * rows, cols),
                (((0,), (0,)), ((), ())),
                preferred_element_type=F32,
            )
            total = term if total is None else total + term
        return total

    def give_share(chunk):
        outputs(wsend, chunk)[...] = product(chunk, 1 - y).astype(BF16)
        send(outputs(wsend, chunk), outputs(winbox, chunk), share_send.at[chunk], share_recv.at[chunk], t, across)

    def keep_share(chunk):
        outputs(wsum_ref, chunk)[...] = product(chunk, y)

    def hop(phase, k, then):
        for chunk in phases[phase]:
            for d in range(2):
                @pl.when(k < came[d])
                def _():
                    here = piece(origin(d, k), c, chunk)
                    done(here, line_recv.at[d, k, chunk])

                    @pl.when(goes[d])
                    def _():
                        send(here, here, line_send.at[d, k + 1, chunk], line_recv.at[d, k + 1, chunk], t, ahead[d])

                    send(here, here, sib_send.at[d, k, chunk], sib_recv.at[d, k, chunk], t, sibling)

            for d in range(2):
                @pl.when(k < came[d])
                def _():
                    done(piece(origin(d, k), 1 - c, chunk), sib_recv.at[d, k, chunk])

            then(chunk)

    def gather(k, carry):
        hop(0, k, lambda chunk: None)

        @pl.when(jnp.logical_and(k == 0, odd))
        def _():
            done(guest, swap.at[1])
            give_columns(guest, near)

        for d in range(2):
            @pl.when(k == came[d])
            def _():
                @pl.when(odd)
                def _():
                    give_columns(guest, beyond[d])

                @pl.when(jnp.logical_not(odd))
                def _():
                    give_columns(cols_ref, beyond[d])

                give_own(d, 1)

        @pl.when(k == min(1, last - 1))
        def _():
            pass_columns(z)
            each(0, pass_columns)

        return carry

    lax.fori_loop(0, last, gather, 0)

    def rest(i, carry):
        each(i, pass_columns)
        return carry

    lax.fori_loop(1, last, rest, 0)
    along(lambda i, bb: done(smalls.at[i], small_recv.at[i]))
    half_ref[...] = jnp.sum(smalls[...], axis=0)
    send(half_ref, away_ref, away_sem.at[0], away_sem.at[1], t, across)
    done(held.at[z, core_rows(1 - c), :], own_sem.at[1])

    def finish(k, carry):
        def then(chunk):
            if chunk < chunks - 1:
                @pl.when(k == last - 1)
                def _():
                    give_share(chunk)

        hop(1, k, then)

        @pl.when(k == 0)
        def _():
            take_columns()
            for chunk in early:
                give_share(chunk)
            done(wbf.at[1 - y], w_sem.at[1])
            multiply(z)

        each(k, multiply)

        @pl.when(k == last - 1)
        def _():
            give_share(chunks - 1)

        @pl.when(k == min(1, last - 1))
        def _():
            give_sum(z)

        @pl.when(k > 0)
        def _():
            each(k - 1, give_sum)

        @pl.when(k == 2)
        def _():
            pass_sum(z)

        @pl.when(k > 1)
        def _():
            each(k - 2, pass_sum)

        return carry

    lax.fori_loop(0, last, finish, 0)
    each(last - 1, give_sum)
    for chunk in early:
        keep_share(chunk)
    if last < 3:
        pass_sum(z)
    if last > 1:
        each(last - 2, pass_sum)
    for chunk in late:
        keep_share(chunk)
    each(last - 1, pass_sum)
    keeps = []
    for chunk in range(chunks):
        done(outputs(winbox, chunk), share_recv.at[chunk])
        outputs(wsum_ref, chunk)[...] += outputs(winbox, chunk)[...].astype(F32)
        keeps.append(pltpu.make_async_copy(outputs(wsum_ref, chunk), outputs(wsum_out, chunk), out_sem.at[chunk]))
        keeps[-1].start()
    done(away_ref, away_sem.at[1])
    total_ref[...] = half_ref[...] + away_ref[...]
    for keep in keeps:
        keep.wait()

    along(lambda i, bb: done(small_ref, small_send.at[i]))
    done(half_ref, away_sem.at[0])
    done(own_rows, own_sem.at[0])
    done(wbf.at[y], w_sem.at[0])
    for chunk in range(chunks):
        done(outputs(wsend, chunk), share_send.at[chunk])

    @pl.when(odd)
    def _():
        done(cols_ref, swap.at[0])

    def sent_columns(j, carry):
        @pl.when(target(j) != b)
        def _():
            done(features(cols_ref, j), x_send.at[j])

        return carry

    lax.fori_loop(0, per, sent_columns, 0)

    def sent_line(zz, carry):
        for yy in range(2):
            done(xblock(yy, zz, lands), x_on.at[yy, zz])

            @pl.when(device(zz, y, t) != b)
            def _():
                done(summed.at[zz, yy], sum_send.at[zz, yy])

        done(theirs.at[zz], pair_send.at[zz])
        return carry

    lax.fori_loop(0, nz, sent_line, 0)

    def back(j, carry):
        done(features(ret_ref, j), ret_recv.at[j])

        @pl.when(c == t)
        def _():
            done(layover.at[j], lay_send.at[j])

        return carry

    lax.fori_loop(0, per, back, 0)

    def sent_pieces(k, carry):
        for chunk in range(chunks):
            for d in range(2):
                @pl.when(jnp.logical_and(goes[d], k <= came[d]))
                def _():
                    done(piece(z, c, chunk), line_send.at[d, k, chunk])

                @pl.when(k < came[d])
                def _():
                    done(piece(z, c, chunk), sib_send.at[d, k, chunk])

        return carry

    lax.fori_loop(0, last, sent_pieces, 0)


def run_exchange(nb, x_first, pre_act, cotangent, gamma, columns, weight):
    rows, outs = x_first.shape
    cols = weight.shape[1]
    nz, per = nb // 4, nb // 2
    last = nz - 1
    phases, cuts = ((0, 1), (2, 3)), tuple(outs * i // 4 for i in range(5))
    chunks = len(cuts) - 1
    dma = pltpu.SemaphoreType.DMA
    vmem = pl.BlockSpec(memory_space=pltpu.VMEM)
    far = pl.BlockSpec(memory_space=pl.ANY)
    return pl.pallas_call(
        functools.partial(exchange, nb, phases, cuts),
        out_shape=(
            jax.ShapeDtypeStruct((outs, cols), F32),
            jax.ShapeDtypeStruct(columns.shape, BF16),
            jax.ShapeDtypeStruct((2, outs), F32),
        ),
        in_specs=[far, far, far, vmem, far, far],
        out_specs=(far, far, vmem),
        scratch_shapes=[
            pltpu.VMEM((rows, outs), BF16),
            pltpu.VMEM((rows, outs), BF16),
            pltpu.VMEM((rows, outs), BF16),
            pltpu.VMEM((outs, cols), F32),
            pltpu.VMEM((nz, 2 * rows, outs), BF16),
            pltpu.VMEM((2, nz, 2 * rows, cols), BF16),
            pltpu.VMEM((nz, 2, rows, cols), F32),
            pltpu.VMEM((nz, 2, rows, cols), BF16),
            pltpu.VMEM((nz, 2, rows, cols), BF16),
            pltpu.VMEM((nz, 2, rows, cols), BF16),
            pltpu.VMEM((per, rows, cols), BF16),
            pltpu.VMEM(columns.shape, BF16),
            pltpu.VMEM((2, outs), F32),
            pltpu.VMEM((2 * nz, 2, outs), F32),
            pltpu.VMEM((2, outs), F32),
            pltpu.VMEM((2, outs), F32),
            pltpu.VMEM((outs, cols), F32),
            pltpu.VMEM((2, outs, cols), BF16),
            pltpu.VMEM((outs, cols), BF16),
            pltpu.VMEM((outs, cols), BF16),
            dma((2, last, chunks)),
            dma((2, last, chunks)),
            dma((2, last, chunks)),
            dma((2, last, chunks)),
            dma((2,)),
            dma((2,)),
            dma((per,)),
            dma((2, nz)),
            dma((2, nz, 2)),
            dma((2,)),
            dma((nz,)),
            dma((nz,)),
            dma((nz, 2)),
            dma((per,)),
            dma((per,)),
            dma((per,)),
            dma((2 * nz,)),
            dma((2 * nz,)),
            dma((2,)),
            dma((chunks,)),
            dma((chunks,)),
            dma((4,)),
            dma((chunks,)),
        ],
        compiler_params=pltpu.CompilerParams(
            collective_id=0, has_side_effects=True, vmem_limit_bytes=60 * 1024 * 1024
        ),
    )(x_first, pre_act, cotangent, gamma, columns, weight)


def results(act_ref, cot_ref, gamma_ref, share_ref, wsum_ref, total_ref, first_ref, layer_ref, weight_ref, bias_ref, sharp_ref):
    act = act_ref[...].astype(F32)
    cot = cot_ref[...].astype(F32)
    first_ref[...] = (cot * (act * jnp.tanh(gamma_ref[...] * act))).astype(BF16)
    layer_ref[...] = (cot + share_ref[...].astype(F32)).astype(BF16)
    weight_ref[...] = wsum_ref[...]
    bias_ref[...] = total_ref[0:1, :]
    sharp_ref[...] = total_ref[1:2, :]


def write_results(pre_act, cotangent, gamma, share, wsum, total):
    rows, outs = pre_act.shape
    cols = wsum.shape[1]
    steps = 2 if rows % 32 == 0 and outs % 16 == 0 else 1
    some = pl.BlockSpec((rows // steps, outs), lambda i: (i, 0))
    tile = pl.BlockSpec((outs // steps, cols), lambda i: (i, 0))
    whole = lambda n: pl.BlockSpec((n, outs), lambda i: (0, 0))
    wide = jax.ShapeDtypeStruct((rows, outs), BF16)
    flat = jax.ShapeDtypeStruct((1, outs), F32)
    return pl.pallas_call(
        results,
        grid=(steps,),
        out_shape=(wide, wide, jax.ShapeDtypeStruct((outs, cols), F32), flat, flat),
        in_specs=[some, some, whole(1), some, tile, whole(2)],
        out_specs=(some, some, tile, whole(1), whole(1)),
    )(pre_act, cotangent, gamma, share, wsum, total)


def shards(nb, x_first, x_layer, pre_act, gamma, weight, cotangent):
    rows = x_layer.shape[0]
    per, cols = nb // 2, weight.shape[1]
    aligned = cols % 128 == 0
    columns = x_layer if aligned else x_layer.reshape(rows, per, cols).transpose(1, 0, 2)
    wsum, share, total = run_exchange(nb, x_first, pre_act, cotangent, gamma[None], columns, weight)
    if not aligned:
        share = share.transpose(1, 0, 2).reshape(rows, per * cols)
    first, layer, grad_weight, bias, sharp = write_results(pre_act, cotangent, gamma[None], share, wsum, total)
    return (first, layer, grad_weight, bias[0], sharp[0])


def solution(mesh):
    assert mesh.shape["table"] == 2 and mesh.shape["batch"] % 8 == 0
    placed = (
        P("batch", "table"),
        P("batch", "table"),
        P("batch", "table"),
        P("table"),
        P("table", "batch"),
        P("batch", "table"),
    )
    return jax.shard_map(
        functools.partial(shards, mesh.shape["batch"]),
        mesh=mesh,
        in_specs=placed,
        out_specs=(
            P("batch", "table"),
            P("batch", "table"),
            P("table", "batch"),
            P("table"),
            P("table"),
        ),
        check_vma=False,
    )
```

```python
import functools

import jax
import jax.numpy as jnp
from jax import lax
from jax.experimental import pallas as pl
from jax.experimental.pallas import tpu as pltpu
from jax.sharding import PartitionSpec as P

MESH = pl.DeviceIdType.MESH
F32 = jnp.float32
BF16 = jnp.bfloat16


def exchange(
    nb, phases, cuts,
    x_in, act_in, cot_in, gamma_ref, cols_ref, weight_ref,
    wsum_out, ret_ref, total_ref,
    x_ref, act_ref, cot_ref, wsum_ref, held, xall, mine, theirs, inbox, summed, layover, guest, small_ref, smalls, half_ref, away_ref,
    wfull, wbf, wsend, winbox,
    line_send, line_recv, sib_send, sib_recv, own_sem, w_sem, x_send, x_on, x_recv, swap,
    pair_send, pair_recv, sum_send, lay_recv, lay_send, ret_recv, small_send, small_recv, away_sem,
    share_send, share_recv, load_sem, out_sem,
):
    rows, outs = x_ref.shape
    cols = wfull.shape[1]
    nz, per = nb // 4, nb // 2
    hz, last = nz // 2, nz - 1
    chunks = len(cuts) - 1
    wide = [cuts[i + 1] - cuts[i] for i in range(chunks)]
    early, late = phases[0], phases[1]
    t, b = lax.axis_index("table"), lax.axis_index("batch")
    z, y, c = b // 4, (b // 2) % 2, b % 2
    other = 1 - t
    home = z // hz

    def device(zz, yy, cc):
        return (zz * 2 + yy) * 2 + cc

    def column(zz, yy, cc):
        return ((zz % hz) * 2 + yy) * 2 + cc

    sibling, across = device(z, y, 1 - c), device(z, 1 - y, c)
    came = (z, last - z)
    goes = (z < last, z > 0)
    ahead = (b + 4, b - 4)

    def origin(d, k):
        return z - 1 - k if d == 0 else z + 1 + k

    def core_rows(core):
        return pl.ds(pl.multiple_of(core * rows, rows), rows)

    def piece(zz, core, chunk):
        return held.at[zz, core_rows(core), pl.ds(cuts[chunk], wide[chunk])]

    def outputs(ref, chunk):
        return ref.at[pl.ds(cuts[chunk], wide[chunk]), :]

    def xblock(yy, zz, core):
        return xall.at[yy, zz, core_rows(core), :]

    def features(ref, j):
        return ref.at[j] if len(ref.shape) == 3 else ref.at[:, pl.ds(pl.multiple_of(j * cols, cols), cols)]

    def done(ref, sem):
        pltpu.make_async_copy(ref, ref, sem).wait()

    def send(src, dst, ssem, rsem, tt, bb):
        return pltpu.make_async_remote_copy(
            src_ref=src, dst_ref=dst, send_sem=ssem, recv_sem=rsem, device_id=(tt, bb), device_id_type=MESH
        ).start()

    def each(k, act):
        for d in range(2):
            @pl.when(k < came[d])
            def _():
                act(origin(d, k))

    barrier = pltpu.get_barrier_semaphore()

    def greet(tt, bb):
        pl.semaphore_signal(barrier, inc=1, device_id=(tt, bb), device_id_type=MESH)

    greet(other, b)
    greet(t, across)

    def along(act):
        def step(i, carry):
            bb = device(i // 2, y, i % 2)

            @pl.when(bb != b)
            def _():
                act(i, bb)

            return carry

        lax.fori_loop(0, 2 * nz, step, 0)

    along(lambda i, bb: greet(t, bb))
    loads = [
        pltpu.make_async_copy(src, dst, load_sem.at[i])
        for i, (src, dst) in enumerate(((act_in, act_ref), (cot_in, cot_ref), (x_in, x_ref), (weight_ref, wfull)))
    ]
    for load in loads:
        load.start()
    small_ref[...] = jnp.zeros_like(small_ref)
    tall = 16 if rows % 16 == 0 else rows
    lanes = 512 if outs % 512 == 0 else outs

    def gate(i, carry):
        at = pl.ds(pl.multiple_of(i * tall, tall), tall)
        put = pl.ds(pl.multiple_of(c * rows + i * tall, tall), tall)
        for lane in range(0, outs, lanes):
            to = pl.ds(lane, lanes)
            sharp = gamma_ref[:, to]
            act = act_ref[at, to].astype(F32)
            tanh = jnp.tanh(sharp * act)
            hidden = cot_ref[at, to].astype(F32) * x_ref[at, to].astype(F32)
            slope = 1.0 - tanh * tanh
            pre = (hidden * (tanh + sharp * act * slope)).astype(BF16)
            held[z, put, to] = pre
            small_ref[0:1, to] += jnp.sum(pre.astype(F32), axis=0, keepdims=True)
            small_ref[1:2, to] += jnp.sum(hidden * act * act * slope, axis=0, keepdims=True)
        return carry

    def give_own(d, phase):
        @pl.when(goes[d])
        def _():
            for chunk in phases[phase]:
                here = piece(z, c, chunk)
                send(here, here, line_send.at[d, 0, chunk], line_recv.at[d, 0, chunk], t, ahead[d])

    odd = c == 1
    side = jnp.where(odd, other, t)

    def target(j):
        return device(side * hz + j // 4, y, j % 2)

    def give_columns(source, chosen):
        def give(j, carry):
            bb = target(j)
            there = xblock((j // 2) % 2, z, c)
            rsem = x_recv.at[(j // 2) % 2, z, c]

            @pl.when(chosen(side * hz + j // 4))
            def _():
                @pl.when(bb == b)
                def _():
                    pltpu.make_async_copy(features(source, j), there, rsem).start()

                @pl.when(bb != b)
                def _():
                    send(features(source, j), there, x_send.at[j], rsem, t, bb)

            return carry

        lax.fori_loop(0, per, give, 0)

    for load in loads[:3]:
        load.wait()
    lax.fori_loop(0, rows // tall, gate, 0)
    loads[3].wait()
    wbf[y] = wfull[...].astype(BF16)
    smalls[2 * z + c] = small_ref[...]
    pl.semaphore_wait(barrier, 2 * nz + 1)
    give_own(0, 0)
    give_own(1, 0)
    own_rows = held.at[z, core_rows(c), :]
    send(own_rows, own_rows, own_sem.at[0], own_sem.at[1], t, sibling)

    @pl.when(odd)
    def _():
        send(cols_ref, guest, swap.at[0], swap.at[1], other, b)

    send(wbf.at[y], wbf.at[y], w_sem.at[0], w_sem.at[1], t, across)
    near = lambda zz: jnp.logical_and(zz <= z + 1, zz >= z - 1)
    beyond = (lambda zz: zz > z + 1, lambda zz: zz < z - 1)

    along(lambda i, bb: send(small_ref, smalls.at[2 * z + c], small_send.at[i], small_recv.at[2 * z + c], t, bb))
    lands = (home + t) % 2

    def pass_columns(zz):
        for yy in range(2):
            ref = xblock(yy, zz, lands)
            done(ref, x_recv.at[yy, zz, lands])
            send(ref, ref, x_on.at[yy, zz], x_recv.at[yy, zz, lands], other, b)

    def take_columns():
        def step(zz, carry):
            for yy in range(2):
                done(xblock(yy, zz, 1 - lands), x_recv.at[yy, zz, 1 - lands])
            return carry

        lax.fori_loop(0, nz, step, 0)

    def half(zz, which, yy):
        return jnp.dot(held[zz, core_rows(which), :], wbf[yy], preferred_element_type=F32)

    def multiply(zz):
        for yy in range(2):
            theirs[zz, yy] = half(zz, other, yy).astype(BF16)
        send(theirs.at[zz], inbox.at[zz], pair_send.at[zz], pair_recv.at[zz], other, b)
        for yy in range(2):
            mine[zz, yy] = half(zz, t, yy)

    def give_sum(zz):
        done(inbox.at[zz], pair_recv.at[zz])
        summed[zz] = (mine[zz] + inbox[zz].astype(F32)).astype(BF16)
        bb = device(zz, y, t)
        for yy in range(2):
            slot = column(z, yy, c)
            for stays, dst, rsem in ((True, ret_ref, ret_recv), (False, layover, lay_recv)):
                right = (home == t) if stays else (home != t)

                @pl.when(jnp.logical_and(right, bb == b))
                def _():
                    pltpu.make_async_copy(summed.at[zz, yy], features(dst, slot), rsem.at[slot]).start()

                @pl.when(jnp.logical_and(right, bb != b))
                def _():
                    send(summed.at[zz, yy], features(dst, slot), sum_send.at[zz, yy], rsem.at[slot], t, bb)

    def pass_sum(zz):
        @pl.when(jnp.logical_and(c == t, zz // hz != t))
        def _():
            for yy in range(2):
                for cc in range(2):
                    j = column(zz, yy, cc)
                    done(layover.at[j], lay_recv.at[j])
                    send(layover.at[j], features(ret_ref, j), lay_send.at[j], ret_recv.at[j], other, b)

    group = 4 if nz % 4 == 0 else nz

    def product(chunk, yy):
        to = pl.ds(cuts[chunk], wide[chunk])
        total = None
        for g in range(0, nz, group):
            zs = pl.ds(g, group)
            term = lax.dot_general(
                held[zs, :, to].reshape(group * 2 * rows, wide[chunk]),
                xall[yy, zs].reshape(group * 2 * rows, cols),
                (((0,), (0,)), ((), ())),
                preferred_element_type=F32,
            )
            total = term if total is None else total + term
        return total

    def give_share(chunk):
        outputs(wsend, chunk)[...] = product(chunk, 1 - y).astype(BF16)
        send(outputs(wsend, chunk), outputs(winbox, chunk), share_send.at[chunk], share_recv.at[chunk], t, across)

    def keep_share(chunk):
        outputs(wsum_ref, chunk)[...] = product(chunk, y)

    def hop(phase, k, then):
        for chunk in phases[phase]:
            for d in range(2):
                @pl.when(k < came[d])
                def _():
                    here = piece(origin(d, k), c, chunk)
                    done(here, line_recv.at[d, k, chunk])

                    @pl.when(goes[d])
                    def _():
                        send(here, here, line_send.at[d, k + 1, chunk], line_recv.at[d, k + 1, chunk], t, ahead[d])

                    send(here, here, sib_send.at[d, k, chunk], sib_recv.at[d, k, chunk], t, sibling)

            for d in range(2):
                @pl.when(k < came[d])
                def _():
                    done(piece(origin(d, k), 1 - c, chunk), sib_recv.at[d, k, chunk])

            then(chunk)

    def gather(k, carry):
        hop(0, k, lambda chunk: None)

        @pl.when(jnp.logical_and(k == 0, odd))
        def _():
            done(guest, swap.at[1])
            give_columns(guest, near)

        @pl.when(jnp.logical_and(k == 0, jnp.logical_not(odd)))
        def _():
            give_columns(cols_ref, near)

        for d in range(2):
            @pl.when(k == jnp.maximum(came[d], min(1, last - 1)))
            def _():
                @pl.when(odd)
                def _():
                    give_columns(guest, beyond[d])

                @pl.when(jnp.logical_not(odd))
                def _():
                    give_columns(cols_ref, beyond[d])

            @pl.when(k == came[d])
            def _():
                give_own(d, 1)

        @pl.when(k == min(1, last - 1))
        def _():
            pass_columns(z)
            each(0, pass_columns)

        return carry

    lax.fori_loop(0, last, gather, 0)

    def rest(i, carry):
        each(i, pass_columns)
        return carry

    lax.fori_loop(1, last, rest, 0)
    along(lambda i, bb: done(smalls.at[i], small_recv.at[i]))
    half_ref[...] = jnp.sum(smalls[...], axis=0)
    send(half_ref, away_ref, away_sem.at[0], away_sem.at[1], t, across)
    done(held.at[z, core_rows(1 - c), :], own_sem.at[1])

    done(wbf.at[1 - y], w_sem.at[1])
    multiply(z)

    def finish(k, carry):
        def then(chunk):
            if chunk < chunks - 1:
                @pl.when(k == last - 1)
                def _():
                    give_share(chunk)

        hop(1, k, then)

        @pl.when(k == 0)
        def _():
            take_columns()
            for chunk in early:
                give_share(chunk)

        each(k, multiply)

        @pl.when(k == last - 1)
        def _():
            give_share(chunks - 1)

        @pl.when(k == min(1, last - 1))
        def _():
            give_sum(z)

        @pl.when(k > 0)
        def _():
            each(k - 1, give_sum)

        @pl.when(k == 2)
        def _():
            pass_sum(z)

        @pl.when(k > 1)
        def _():
            each(k - 2, pass_sum)

        return carry

    lax.fori_loop(0, last, finish, 0)
    each(last - 1, give_sum)
    for chunk in early:
        keep_share(chunk)
    if last < 3:
        pass_sum(z)
    if last > 1:
        each(last - 2, pass_sum)
    for chunk in late:
        keep_share(chunk)
    each(last - 1, pass_sum)
    keeps = []
    for chunk in range(chunks):
        done(outputs(winbox, chunk), share_recv.at[chunk])
        outputs(wsum_ref, chunk)[...] += outputs(winbox, chunk)[...].astype(F32)
        keeps.append(pltpu.make_async_copy(outputs(wsum_ref, chunk), outputs(wsum_out, chunk), out_sem.at[chunk]))
        keeps[-1].start()
    done(away_ref, away_sem.at[1])
    total_ref[...] = half_ref[...] + away_ref[...]
    for keep in keeps:
        keep.wait()

    along(lambda i, bb: done(small_ref, small_send.at[i]))
    done(half_ref, away_sem.at[0])
    done(own_rows, own_sem.at[0])
    done(wbf.at[y], w_sem.at[0])
    for chunk in range(chunks):
        done(outputs(wsend, chunk), share_send.at[chunk])

    @pl.when(odd)
    def _():
        done(cols_ref, swap.at[0])

    def sent_columns(j, carry):
        @pl.when(target(j) != b)
        def _():
            done(features(cols_ref, j), x_send.at[j])

        return carry

    lax.fori_loop(0, per, sent_columns, 0)

    def sent_line(zz, carry):
        for yy in range(2):
            done(xblock(yy, zz, lands), x_on.at[yy, zz])

            @pl.when(device(zz, y, t) != b)
            def _():
                done(summed.at[zz, yy], sum_send.at[zz, yy])

        done(theirs.at[zz], pair_send.at[zz])
        return carry

    lax.fori_loop(0, nz, sent_line, 0)

    def back(j, carry):
        done(features(ret_ref, j), ret_recv.at[j])

        @pl.when(c == t)
        def _():
            done(layover.at[j], lay_send.at[j])

        return carry

    lax.fori_loop(0, per, back, 0)

    def sent_pieces(k, carry):
        for chunk in range(chunks):
            for d in range(2):
                @pl.when(jnp.logical_and(goes[d], k <= came[d]))
                def _():
                    done(piece(z, c, chunk), line_send.at[d, k, chunk])

                @pl.when(k < came[d])
                def _():
                    done(piece(z, c, chunk), sib_send.at[d, k, chunk])

        return carry

    lax.fori_loop(0, last, sent_pieces, 0)


def run_exchange(nb, x_first, pre_act, cotangent, gamma, columns, weight):
    rows, outs = x_first.shape
    cols = weight.shape[1]
    nz, per = nb // 4, nb // 2
    last = nz - 1
    phases, cuts = ((0, 1), (2, 3)), tuple(outs * i // 4 for i in range(5))
    chunks = len(cuts) - 1
    dma = pltpu.SemaphoreType.DMA
    vmem = pl.BlockSpec(memory_space=pltpu.VMEM)
    far = pl.BlockSpec(memory_space=pl.ANY)
    return pl.pallas_call(
        functools.partial(exchange, nb, phases, cuts),
        out_shape=(
            jax.ShapeDtypeStruct((outs, cols), F32),
            jax.ShapeDtypeStruct(columns.shape, BF16),
            jax.ShapeDtypeStruct((2, outs), F32),
        ),
        in_specs=[far, far, far, vmem, far, far],
        out_specs=(far, far, vmem),
        scratch_shapes=[
            pltpu.VMEM((rows, outs), BF16),
            pltpu.VMEM((rows, outs), BF16),
            pltpu.VMEM((rows, outs), BF16),
            pltpu.VMEM((outs, cols), F32),
            pltpu.VMEM((nz, 2 * rows, outs), BF16),
            pltpu.VMEM((2, nz, 2 * rows, cols), BF16),
            pltpu.VMEM((nz, 2, rows, cols), F32),
            pltpu.VMEM((nz, 2, rows, cols), BF16),
            pltpu.VMEM((nz, 2, rows, cols), BF16),
            pltpu.VMEM((nz, 2, rows, cols), BF16),
            pltpu.VMEM((per, rows, cols), BF16),
            pltpu.VMEM(columns.shape, BF16),
            pltpu.VMEM((2, outs), F32),
            pltpu.VMEM((2 * nz, 2, outs), F32),
            pltpu.VMEM((2, outs), F32),
            pltpu.VMEM((2, outs), F32),
            pltpu.VMEM((outs, cols), F32),
            pltpu.VMEM((2, outs, cols), BF16),
            pltpu.VMEM((outs, cols), BF16),
            pltpu.VMEM((outs, cols), BF16),
            dma((2, last, chunks)),
            dma((2, last, chunks)),
            dma((2, last, chunks)),
            dma((2, last, chunks)),
            dma((2,)),
            dma((2,)),
            dma((per,)),
            dma((2, nz)),
            dma((2, nz, 2)),
            dma((2,)),
            dma((nz,)),
            dma((nz,)),
            dma((nz, 2)),
            dma((per,)),
            dma((per,)),
            dma((per,)),
            dma((2 * nz,)),
            dma((2 * nz,)),
            dma((2,)),
            dma((chunks,)),
            dma((chunks,)),
            dma((4,)),
            dma((chunks,)),
        ],
        compiler_params=pltpu.CompilerParams(
            collective_id=0, has_side_effects=True, vmem_limit_bytes=60 * 1024 * 1024
        ),
    )(x_first, pre_act, cotangent, gamma, columns, weight)


def results(act_ref, cot_ref, gamma_ref, share_ref, wsum_ref, total_ref, first_ref, layer_ref, weight_ref, bias_ref, sharp_ref):
    act = act_ref[...].astype(F32)
    cot = cot_ref[...].astype(F32)
    first_ref[...] = (cot * (act * jnp.tanh(gamma_ref[...] * act))).astype(BF16)
    layer_ref[...] = (cot + share_ref[...].astype(F32)).astype(BF16)
    weight_ref[...] = wsum_ref[...]
    bias_ref[...] = total_ref[0:1, :]
    sharp_ref[...] = total_ref[1:2, :]


def write_results(pre_act, cotangent, gamma, share, wsum, total):
    rows, outs = pre_act.shape
    cols = wsum.shape[1]
    steps = 2 if rows % 32 == 0 and outs % 16 == 0 else 1
    some = pl.BlockSpec((rows // steps, outs), lambda i: (i, 0))
    tile = pl.BlockSpec((outs // steps, cols), lambda i: (i, 0))
    whole = lambda n: pl.BlockSpec((n, outs), lambda i: (0, 0))
    wide = jax.ShapeDtypeStruct((rows, outs), BF16)
    flat = jax.ShapeDtypeStruct((1, outs), F32)
    return pl.pallas_call(
        results,
        grid=(steps,),
        out_shape=(wide, wide, jax.ShapeDtypeStruct((outs, cols), F32), flat, flat),
        in_specs=[some, some, whole(1), some, tile, whole(2)],
        out_specs=(some, some, tile, whole(1), whole(1)),
    )(pre_act, cotangent, gamma, share, wsum, total)


def shards(nb, x_first, x_layer, pre_act, gamma, weight, cotangent):
    rows = x_layer.shape[0]
    per, cols = nb // 2, weight.shape[1]
    aligned = cols % 128 == 0
    columns = x_layer if aligned else x_layer.reshape(rows, per, cols).transpose(1, 0, 2)
    wsum, share, total = run_exchange(nb, x_first, pre_act, cotangent, gamma[None], columns, weight)
    if not aligned:
        share = share.transpose(1, 0, 2).reshape(rows, per * cols)
    first, layer, grad_weight, bias, sharp = write_results(pre_act, cotangent, gamma[None], share, wsum, total)
    return (first, layer, grad_weight, bias[0], sharp[0])


def solution(mesh):
    assert mesh.shape["table"] == 2 and mesh.shape["batch"] % 8 == 0
    placed = (
        P("batch", "table"),
        P("batch", "table"),
        P("batch", "table"),
        P("table"),
        P("table", "batch"),
        P("batch", "table"),
    )
    return jax.shard_map(
        functools.partial(shards, mesh.shape["batch"]),
        mesh=mesh,
        in_specs=placed,
        out_specs=(
            P("batch", "table"),
            P("batch", "table"),
            P("table", "batch"),
            P("table"),
            P("table"),
        ),
        check_vma=False,
    )
```

```python
import functools

import jax
import jax.numpy as jnp
from jax import lax
from jax.experimental import pallas as pl
from jax.experimental.pallas import tpu as pltpu
from jax.sharding import PartitionSpec as P

MESH = pl.DeviceIdType.MESH
F32 = jnp.float32
BF16 = jnp.bfloat16


def exchange(
    nb, phases, cuts,
    x_in, act_in, cot_in, gamma_ref, cols_ref, weight_ref,
    wsum_out, ret_ref, total_ref,
    x_ref, act_ref, cot_ref, wsum_ref, held, xall, mine, theirs, inbox, summed, layover, guest, small_ref, smalls, half_ref, near_ref, both_ref, away_ref,
    wfull, wbf, wsend, winbox,
    line_send, line_recv, sib_send, sib_recv, own_sem, w_sem, x_send, x_on, x_recv, swap,
    pair_send, pair_recv, sum_send, lay_recv, lay_send, ret_recv, small_send, small_recv, near_sem, away_sem,
    share_send, share_recv, load_sem, out_sem,
):
    rows, outs = x_ref.shape
    cols = wfull.shape[1]
    nz, per = nb // 4, nb // 2
    hz, last = nz // 2, nz - 1
    chunks = len(cuts) - 1
    wide = [cuts[i + 1] - cuts[i] for i in range(chunks)]
    early, late = phases[0], phases[1]
    t, b = lax.axis_index("table"), lax.axis_index("batch")
    z, y, c = b // 4, (b // 2) % 2, b % 2
    other = 1 - t
    home = z // hz

    def device(zz, yy, cc):
        return (zz * 2 + yy) * 2 + cc

    def column(zz, yy, cc):
        return ((zz % hz) * 2 + yy) * 2 + cc

    sibling, across = device(z, y, 1 - c), device(z, 1 - y, c)
    came = (z, last - z)
    goes = (z < last, z > 0)
    ahead = (b + 4, b - 4)

    def origin(d, k):
        return z - 1 - k if d == 0 else z + 1 + k

    def core_rows(core):
        return pl.ds(pl.multiple_of(core * rows, rows), rows)

    def piece(zz, core, chunk):
        return held.at[zz, core_rows(core), pl.ds(cuts[chunk], wide[chunk])]

    def outputs(ref, chunk):
        return ref.at[pl.ds(cuts[chunk], wide[chunk]), :]

    def xblock(yy, zz, core):
        return xall.at[yy, zz, core_rows(core), :]

    def features(ref, j):
        return ref.at[j] if len(ref.shape) == 3 else ref.at[:, pl.ds(pl.multiple_of(j * cols, cols), cols)]

    def done(ref, sem):
        pltpu.make_async_copy(ref, ref, sem).wait()

    def send(src, dst, ssem, rsem, tt, bb):
        return pltpu.make_async_remote_copy(
            src_ref=src, dst_ref=dst, send_sem=ssem, recv_sem=rsem, device_id=(tt, bb), device_id_type=MESH
        ).start()

    def each(k, act):
        for d in range(2):
            @pl.when(k < came[d])
            def _():
                act(origin(d, k))

    barrier = pltpu.get_barrier_semaphore()

    def greet(tt, bb):
        pl.semaphore_signal(barrier, inc=1, device_id=(tt, bb), device_id_type=MESH)

    greet(other, b)
    greet(t, across)

    def along(act):
        def step(i, carry):
            bb = device(i // 2, y, i % 2)

            @pl.when(bb != b)
            def _():
                act(i, bb)

            return carry

        lax.fori_loop(0, 2 * nz, step, 0)

    along(lambda i, bb: greet(t, bb))
    loads = [
        pltpu.make_async_copy(src, dst, load_sem.at[i])
        for i, (src, dst) in enumerate(((act_in, act_ref), (cot_in, cot_ref), (x_in, x_ref), (weight_ref, wfull)))
    ]
    for load in loads:
        load.start()
    small_ref[...] = jnp.zeros_like(small_ref)
    tall = 16 if rows % 16 == 0 else rows
    lanes = 512 if outs % 512 == 0 else outs

    def gate(i, carry):
        at = pl.ds(pl.multiple_of(i * tall, tall), tall)
        put = pl.ds(pl.multiple_of(c * rows + i * tall, tall), tall)
        for lane in range(0, outs, lanes):
            to = pl.ds(lane, lanes)
            sharp = gamma_ref[:, to]
            act = act_ref[at, to].astype(F32)
            tanh = jnp.tanh(sharp * act)
            hidden = cot_ref[at, to].astype(F32) * x_ref[at, to].astype(F32)
            slope = 1.0 - tanh * tanh
            pre = (hidden * (tanh + sharp * act * slope)).astype(BF16)
            held[z, put, to] = pre
            small_ref[0:1, to] += jnp.sum(pre.astype(F32), axis=0, keepdims=True)
            small_ref[1:2, to] += jnp.sum(hidden * act * act * slope, axis=0, keepdims=True)
        return carry

    def give_own(d, phase):
        @pl.when(goes[d])
        def _():
            for chunk in phases[phase]:
                here = piece(z, c, chunk)
                send(here, here, line_send.at[d, 0, chunk], line_recv.at[d, 0, chunk], t, ahead[d])

    odd = c == 1
    side = jnp.where(odd, other, t)

    def target(j):
        return device(side * hz + j // 4, y, j % 2)

    def give_columns(source, chosen):
        def give(j, carry):
            bb = target(j)
            there = xblock((j // 2) % 2, z, c)
            rsem = x_recv.at[(j // 2) % 2, z, c]

            @pl.when(chosen(side * hz + j // 4))
            def _():
                @pl.when(bb == b)
                def _():
                    pltpu.make_async_copy(features(source, j), there, rsem).start()

                @pl.when(bb != b)
                def _():
                    send(features(source, j), there, x_send.at[j], rsem, t, bb)

            return carry

        lax.fori_loop(0, per, give, 0)

    for load in loads[:3]:
        load.wait()
    lax.fori_loop(0, rows // tall, gate, 0)
    loads[3].wait()
    wbf[y] = wfull[...].astype(BF16)
    smalls[z] = small_ref[...]
    pl.semaphore_wait(barrier, 2 * nz + 1)
    give_own(0, 0)
    give_own(1, 0)
    own_rows = held.at[z, core_rows(c), :]
    send(own_rows, own_rows, own_sem.at[0], own_sem.at[1], t, sibling)

    @pl.when(odd)
    def _():
        send(cols_ref, guest, swap.at[0], swap.at[1], other, b)

    send(wbf.at[y], wbf.at[y], w_sem.at[0], w_sem.at[1], t, across)
    near = lambda zz: jnp.logical_and(zz <= z + 1, zz >= z - 1)
    beyond = (lambda zz: zz > z + 1, lambda zz: zz < z - 1)

    def same_core(act):
        def step(zz, carry):
            @pl.when(zz != z)
            def _():
                act(zz, device(zz, y, c))

            return carry

        lax.fori_loop(0, nz, step, 0)

    same_core(lambda zz, bb: send(small_ref, smalls.at[z], small_send.at[zz], small_recv.at[z], t, bb))
    lands = (home + t) % 2

    def pass_columns(zz):
        for yy in range(2):
            ref = xblock(yy, zz, lands)
            done(ref, x_recv.at[yy, zz, lands])
            send(ref, ref, x_on.at[yy, zz], x_recv.at[yy, zz, lands], other, b)

    def take_columns():
        def step(zz, carry):
            for yy in range(2):
                done(xblock(yy, zz, 1 - lands), x_recv.at[yy, zz, 1 - lands])
            return carry

        lax.fori_loop(0, nz, step, 0)

    def half(zz, which, yy):
        return jnp.dot(held[zz, core_rows(which), :], wbf[yy], preferred_element_type=F32)

    def multiply(zz):
        for yy in range(2):
            theirs[zz, yy] = half(zz, other, yy).astype(BF16)
        send(theirs.at[zz], inbox.at[zz], pair_send.at[zz], pair_recv.at[zz], other, b)
        for yy in range(2):
            mine[zz, yy] = half(zz, t, yy)

    def give_sum(zz):
        done(inbox.at[zz], pair_recv.at[zz])
        summed[zz] = (mine[zz] + inbox[zz].astype(F32)).astype(BF16)
        bb = device(zz, y, t)
        for yy in range(2):
            slot = column(z, yy, c)
            for stays, dst, rsem in ((True, ret_ref, ret_recv), (False, layover, lay_recv)):
                right = (home == t) if stays else (home != t)

                @pl.when(jnp.logical_and(right, bb == b))
                def _():
                    pltpu.make_async_copy(summed.at[zz, yy], features(dst, slot), rsem.at[slot]).start()

                @pl.when(jnp.logical_and(right, bb != b))
                def _():
                    send(summed.at[zz, yy], features(dst, slot), sum_send.at[zz, yy], rsem.at[slot], t, bb)

    def pass_sum(zz):
        @pl.when(jnp.logical_and(c == t, zz // hz != t))
        def _():
            for yy in range(2):
                for cc in range(2):
                    j = column(zz, yy, cc)
                    done(layover.at[j], lay_recv.at[j])
                    send(layover.at[j], features(ret_ref, j), lay_send.at[j], ret_recv.at[j], other, b)

    group = 4 if nz % 4 == 0 else nz

    def product(chunk, yy):
        to = pl.ds(cuts[chunk], wide[chunk])
        total = None
        for g in range(0, nz, group):
            zs = pl.ds(g, group)
            term = lax.dot_general(
                held[zs, :, to].reshape(group * 2 * rows, wide[chunk]),
                xall[yy, zs].reshape(group * 2 * rows, cols),
                (((0,), (0,)), ((), ())),
                preferred_element_type=F32,
            )
            total = term if total is None else total + term
        return total

    def give_share(chunk):
        outputs(wsend, chunk)[...] = product(chunk, 1 - y).astype(BF16)
        send(outputs(wsend, chunk), outputs(winbox, chunk), share_send.at[chunk], share_recv.at[chunk], t, across)

    def keep_share(chunk):
        outputs(wsum_ref, chunk)[...] = product(chunk, y)

    def hop(phase, k, then):
        for chunk in phases[phase]:
            for d in range(2):
                @pl.when(k < came[d])
                def _():
                    here = piece(origin(d, k), c, chunk)
                    done(here, line_recv.at[d, k, chunk])

                    @pl.when(goes[d])
                    def _():
                        send(here, here, line_send.at[d, k + 1, chunk], line_recv.at[d, k + 1, chunk], t, ahead[d])

                    send(here, here, sib_send.at[d, k, chunk], sib_recv.at[d, k, chunk], t, sibling)

            for d in range(2):
                @pl.when(k < came[d])
                def _():
                    done(piece(origin(d, k), 1 - c, chunk), sib_recv.at[d, k, chunk])

            then(chunk)

    def gather(k, carry):
        hop(0, k, lambda chunk: None)

        @pl.when(jnp.logical_and(k == 0, odd))
        def _():
            done(guest, swap.at[1])
            give_columns(guest, near)

        @pl.when(jnp.logical_and(k == 0, jnp.logical_not(odd)))
        def _():
            give_columns(cols_ref, near)

        for d in range(2):
            @pl.when(k == jnp.maximum(came[d], min(1, last - 1)))
            def _():
                @pl.when(odd)
                def _():
                    give_columns(guest, beyond[d])

                @pl.when(jnp.logical_not(odd))
                def _():
                    give_columns(cols_ref, beyond[d])

            @pl.when(k == came[d])
            def _():
                give_own(d, 1)

        @pl.when(k == min(1, last - 1))
        def _():
            pass_columns(z)
            each(0, pass_columns)

        return carry

    lax.fori_loop(0, last, gather, 0)

    def rest(i, carry):
        each(i, pass_columns)
        return carry

    lax.fori_loop(1, last, rest, 0)
    same_core(lambda zz, bb: done(smalls.at[zz], small_recv.at[zz]))
    half_ref[...] = jnp.sum(smalls[...], axis=0)
    send(half_ref, near_ref, near_sem.at[0], near_sem.at[1], t, sibling)
    done(held.at[z, core_rows(1 - c), :], own_sem.at[1])

    done(wbf.at[1 - y], w_sem.at[1])
    multiply(z)

    def finish(k, carry):
        def then(chunk):
            if chunk < chunks - 1:
                @pl.when(k == last - 1)
                def _():
                    give_share(chunk)

        hop(1, k, then)

        @pl.when(k == 0)
        def _():
            take_columns()
            for chunk in early:
                give_share(chunk)

        each(k, multiply)

        @pl.when(k == last - 1)
        def _():
            give_share(chunks - 1)

        @pl.when(k == min(1, last - 1))
        def _():
            give_sum(z)

        @pl.when(k > 0)
        def _():
            each(k - 1, give_sum)

        @pl.when(k == 2)
        def _():
            pass_sum(z)

        @pl.when(k > 1)
        def _():
            each(k - 2, pass_sum)

        return carry

    lax.fori_loop(0, last, finish, 0)
    done(near_ref, near_sem.at[1])
    both_ref[...] = half_ref[...] + near_ref[...]
    send(both_ref, away_ref, away_sem.at[0], away_sem.at[1], t, across)
    each(last - 1, give_sum)
    for chunk in early:
        keep_share(chunk)
    if last < 3:
        pass_sum(z)
    if last > 1:
        each(last - 2, pass_sum)
    for chunk in late:
        keep_share(chunk)
    each(last - 1, pass_sum)
    keeps = []
    for chunk in range(chunks):
        done(outputs(winbox, chunk), share_recv.at[chunk])
        outputs(wsum_ref, chunk)[...] += outputs(winbox, chunk)[...].astype(F32)
        keeps.append(pltpu.make_async_copy(outputs(wsum_ref, chunk), outputs(wsum_out, chunk), out_sem.at[chunk]))
        keeps[-1].start()
    done(away_ref, away_sem.at[1])
    total_ref[...] = both_ref[...] + away_ref[...]
    for keep in keeps:
        keep.wait()

    same_core(lambda zz, bb: done(small_ref, small_send.at[zz]))
    done(half_ref, near_sem.at[0])
    done(both_ref, away_sem.at[0])
    done(own_rows, own_sem.at[0])
    done(wbf.at[y], w_sem.at[0])
    for chunk in range(chunks):
        done(outputs(wsend, chunk), share_send.at[chunk])

    @pl.when(odd)
    def _():
        done(cols_ref, swap.at[0])

    def sent_columns(j, carry):
        @pl.when(target(j) != b)
        def _():
            done(features(cols_ref, j), x_send.at[j])

        return carry

    lax.fori_loop(0, per, sent_columns, 0)

    def sent_line(zz, carry):
        for yy in range(2):
            done(xblock(yy, zz, lands), x_on.at[yy, zz])

            @pl.when(device(zz, y, t) != b)
            def _():
                done(summed.at[zz, yy], sum_send.at[zz, yy])

        done(theirs.at[zz], pair_send.at[zz])
        return carry

    lax.fori_loop(0, nz, sent_line, 0)

    def back(j, carry):
        done(features(ret_ref, j), ret_recv.at[j])

        @pl.when(c == t)
        def _():
            done(layover.at[j], lay_send.at[j])

        return carry

    lax.fori_loop(0, per, back, 0)

    def sent_pieces(k, carry):
        for chunk in range(chunks):
            for d in range(2):
                @pl.when(jnp.logical_and(goes[d], k <= came[d]))
                def _():
                    done(piece(z, c, chunk), line_send.at[d, k, chunk])

                @pl.when(k < came[d])
                def _():
                    done(piece(z, c, chunk), sib_send.at[d, k, chunk])

        return carry

    lax.fori_loop(0, last, sent_pieces, 0)


def run_exchange(nb, x_first, pre_act, cotangent, gamma, columns, weight):
    rows, outs = x_first.shape
    cols = weight.shape[1]
    nz, per = nb // 4, nb // 2
    last = nz - 1
    phases, cuts = ((0, 1), (2, 3)), tuple(outs * i // 4 for i in range(5))
    chunks = len(cuts) - 1
    dma = pltpu.SemaphoreType.DMA
    vmem = pl.BlockSpec(memory_space=pltpu.VMEM)
    far = pl.BlockSpec(memory_space=pl.ANY)
    return pl.pallas_call(
        functools.partial(exchange, nb, phases, cuts),
        out_shape=(
            jax.ShapeDtypeStruct((outs, cols), F32),
            jax.ShapeDtypeStruct(columns.shape, BF16),
            jax.ShapeDtypeStruct((2, outs), F32),
        ),
        in_specs=[far, far, far, vmem, far, far],
        out_specs=(far, far, vmem),
        scratch_shapes=[
            pltpu.VMEM((rows, outs), BF16),
            pltpu.VMEM((rows, outs), BF16),
            pltpu.VMEM((rows, outs), BF16),
            pltpu.VMEM((outs, cols), F32),
            pltpu.VMEM((nz, 2 * rows, outs), BF16),
            pltpu.VMEM((2, nz, 2 * rows, cols), BF16),
            pltpu.VMEM((nz, 2, rows, cols), F32),
            pltpu.VMEM((nz, 2, rows, cols), BF16),
            pltpu.VMEM((nz, 2, rows, cols), BF16),
            pltpu.VMEM((nz, 2, rows, cols), BF16),
            pltpu.VMEM((per, rows, cols), BF16),
            pltpu.VMEM(columns.shape, BF16),
            pltpu.VMEM((2, outs), F32),
            pltpu.VMEM((nz, 2, outs), F32),
            pltpu.VMEM((2, outs), F32),
            pltpu.VMEM((2, outs), F32),
            pltpu.VMEM((2, outs), F32),
            pltpu.VMEM((2, outs), F32),
            pltpu.VMEM((outs, cols), F32),
            pltpu.VMEM((2, outs, cols), BF16),
            pltpu.VMEM((outs, cols), BF16),
            pltpu.VMEM((outs, cols), BF16),
            dma((2, last, chunks)),
            dma((2, last, chunks)),
            dma((2, last, chunks)),
            dma((2, last, chunks)),
            dma((2,)),
            dma((2,)),
            dma((per,)),
            dma((2, nz)),
            dma((2, nz, 2)),
            dma((2,)),
            dma((nz,)),
            dma((nz,)),
            dma((nz, 2)),
            dma((per,)),
            dma((per,)),
            dma((per,)),
            dma((nz,)),
            dma((nz,)),
            dma((2,)),
            dma((2,)),
            dma((chunks,)),
            dma((chunks,)),
            dma((4,)),
            dma((chunks,)),
        ],
        compiler_params=pltpu.CompilerParams(
            collective_id=0, has_side_effects=True, vmem_limit_bytes=60 * 1024 * 1024
        ),
    )(x_first, pre_act, cotangent, gamma, columns, weight)


def results(act_ref, cot_ref, gamma_ref, share_ref, wsum_ref, total_ref, first_ref, layer_ref, weight_ref, bias_ref, sharp_ref):
    act = act_ref[...].astype(F32)
    cot = cot_ref[...].astype(F32)
    first_ref[...] = (cot * (act * jnp.tanh(gamma_ref[...] * act))).astype(BF16)
    layer_ref[...] = (cot + share_ref[...].astype(F32)).astype(BF16)
    weight_ref[...] = wsum_ref[...]
    bias_ref[...] = total_ref[0:1, :]
    sharp_ref[...] = total_ref[1:2, :]


def write_results(pre_act, cotangent, gamma, share, wsum, total):
    rows, outs = pre_act.shape
    cols = wsum.shape[1]
    steps = 2 if rows % 32 == 0 and outs % 16 == 0 else 1
    some = pl.BlockSpec((rows // steps, outs), lambda i: (i, 0))
    tile = pl.BlockSpec((outs // steps, cols), lambda i: (i, 0))
    whole = lambda n: pl.BlockSpec((n, outs), lambda i: (0, 0))
    wide = jax.ShapeDtypeStruct((rows, outs), BF16)
    flat = jax.ShapeDtypeStruct((1, outs), F32)
    return pl.pallas_call(
        results,
        grid=(steps,),
        out_shape=(wide, wide, jax.ShapeDtypeStruct((outs, cols), F32), flat, flat),
        in_specs=[some, some, whole(1), some, tile, whole(2)],
        out_specs=(some, some, tile, whole(1), whole(1)),
    )(pre_act, cotangent, gamma, share, wsum, total)


def shards(nb, x_first, x_layer, pre_act, gamma, weight, cotangent):
    rows = x_layer.shape[0]
    per, cols = nb // 2, weight.shape[1]
    aligned = cols % 128 == 0
    columns = x_layer if aligned else x_layer.reshape(rows, per, cols).transpose(1, 0, 2)
    wsum, share, total = run_exchange(nb, x_first, pre_act, cotangent, gamma[None], columns, weight)
    if not aligned:
        share = share.transpose(1, 0, 2).reshape(rows, per * cols)
    first, layer, grad_weight, bias, sharp = write_results(pre_act, cotangent, gamma[None], share, wsum, total)
    return (first, layer, grad_weight, bias[0], sharp[0])


def solution(mesh):
    assert mesh.shape["table"] == 2 and mesh.shape["batch"] % 8 == 0
    placed = (
        P("batch", "table"),
        P("batch", "table"),
        P("batch", "table"),
        P("table"),
        P("table", "batch"),
        P("batch", "table"),
    )
    return jax.shard_map(
        functools.partial(shards, mesh.shape["batch"]),
        mesh=mesh,
        in_specs=placed,
        out_specs=(
            P("batch", "table"),
            P("batch", "table"),
            P("table", "batch"),
            P("table"),
            P("table"),
        ),
        check_vma=False,
    )
```

```python
import functools

import jax
import jax.numpy as jnp
from jax import lax
from jax.experimental import pallas as pl
from jax.experimental.pallas import tpu as pltpu
from jax.sharding import PartitionSpec as P

MESH = pl.DeviceIdType.MESH
F32 = jnp.float32
BF16 = jnp.bfloat16


def exchange(
    nb, phases, cuts,
    x_in, act_in, cot_in, gamma_ref, cols_ref, weight_ref,
    wsum_out, ret_ref, total_ref,
    x_ref, act_ref, cot_ref, wsum_ref, held, xall, mine, theirs, inbox, summed, layover, guest, small_ref, smalls, half_ref, near_ref, both_ref, away_ref,
    wfull, wbf, wsend, winbox,
    line_send, line_recv, sib_send, sib_recv, own_sem, w_sem, x_send, x_on, x_recv, swap,
    pair_send, pair_recv, sum_send, lay_recv, lay_send, ret_recv, small_send, small_recv, near_sem, away_sem,
    share_send, share_recv, load_sem, out_sem,
):
    rows, outs = x_ref.shape
    cols = wfull.shape[1]
    nz, per = nb // 4, nb // 2
    hz, last = nz // 2, nz - 1
    chunks = len(cuts) - 1
    wide = [cuts[i + 1] - cuts[i] for i in range(chunks)]
    early, late = phases[0], phases[1]
    t, b = lax.axis_index("table"), lax.axis_index("batch")
    z, y, c = b // 4, (b // 2) % 2, b % 2
    other = 1 - t
    home = z // hz

    def device(zz, yy, cc):
        return (zz * 2 + yy) * 2 + cc

    def column(zz, yy, cc):
        return ((zz % hz) * 2 + yy) * 2 + cc

    sibling, across = device(z, y, 1 - c), device(z, 1 - y, c)
    came = (z, last - z)
    goes = (z < last, z > 0)
    ahead = (b + 4, b - 4)

    def origin(d, k):
        return z - 1 - k if d == 0 else z + 1 + k

    def core_rows(core):
        return pl.ds(pl.multiple_of(core * rows, rows), rows)

    def piece(zz, core, chunk):
        return held.at[zz, core_rows(core), pl.ds(cuts[chunk], wide[chunk])]

    def outputs(ref, chunk):
        return ref.at[pl.ds(cuts[chunk], wide[chunk]), :]

    def xblock(yy, zz, core):
        return xall.at[yy, zz, core_rows(core), :]

    def features(ref, j):
        return ref.at[j] if len(ref.shape) == 3 else ref.at[:, pl.ds(pl.multiple_of(j * cols, cols), cols)]

    def done(ref, sem):
        pltpu.make_async_copy(ref, ref, sem).wait()

    def send(src, dst, ssem, rsem, tt, bb):
        return pltpu.make_async_remote_copy(
            src_ref=src, dst_ref=dst, send_sem=ssem, recv_sem=rsem, device_id=(tt, bb), device_id_type=MESH
        ).start()

    def each(k, act):
        for d in range(2):
            @pl.when(k < came[d])
            def _():
                act(origin(d, k))

    barrier = pltpu.get_barrier_semaphore()

    def greet(tt, bb):
        pl.semaphore_signal(barrier, inc=1, device_id=(tt, bb), device_id_type=MESH)

    greet(other, b)
    greet(t, across)

    def along(act):
        def step(i, carry):
            bb = device(i // 2, y, i % 2)

            @pl.when(bb != b)
            def _():
                act(i, bb)

            return carry

        lax.fori_loop(0, 2 * nz, step, 0)

    along(lambda i, bb: greet(t, bb))
    loads = [
        pltpu.make_async_copy(src, dst, load_sem.at[i])
        for i, (src, dst) in enumerate(((act_in, act_ref), (cot_in, cot_ref), (x_in, x_ref), (weight_ref, wfull)))
    ]
    for load in loads:
        load.start()
    small_ref[...] = jnp.zeros_like(small_ref)
    tall = 16 if rows % 16 == 0 else rows
    lanes = 512 if outs % 512 == 0 else outs

    def gate(i, carry):
        at = pl.ds(pl.multiple_of(i * tall, tall), tall)
        put = pl.ds(pl.multiple_of(c * rows + i * tall, tall), tall)
        for lane in range(0, outs, lanes):
            to = pl.ds(lane, lanes)
            sharp = gamma_ref[:, to]
            act = act_ref[at, to].astype(F32)
            tanh = jnp.tanh(sharp * act)
            hidden = cot_ref[at, to].astype(F32) * x_ref[at, to].astype(F32)
            slope = 1.0 - tanh * tanh
            pre = (hidden * (tanh + sharp * act * slope)).astype(BF16)
            held[z, put, to] = pre
            small_ref[0:1, to] += jnp.sum(pre.astype(F32), axis=0, keepdims=True)
            small_ref[1:2, to] += jnp.sum(hidden * act * act * slope, axis=0, keepdims=True)
        return carry

    def give_own(d, phase):
        @pl.when(goes[d])
        def _():
            for chunk in phases[phase]:
                here = piece(z, c, chunk)
                send(here, here, line_send.at[d, 0, chunk], line_recv.at[d, 0, chunk], t, ahead[d])

    odd = c == 1
    side = jnp.where(odd, other, t)

    def target(j):
        return device(side * hz + j // 4, y, j % 2)

    def give_columns(source, chosen):
        def give(j, carry):
            bb = target(j)
            there = xblock((j // 2) % 2, z, c)
            rsem = x_recv.at[(j // 2) % 2, z, c]

            @pl.when(chosen(side * hz + j // 4))
            def _():
                @pl.when(bb == b)
                def _():
                    pltpu.make_async_copy(features(source, j), there, rsem).start()

                @pl.when(bb != b)
                def _():
                    send(features(source, j), there, x_send.at[j], rsem, t, bb)

            return carry

        lax.fori_loop(0, per, give, 0)

    for load in loads[:3]:
        load.wait()
    lax.fori_loop(0, rows // tall, gate, 0)
    loads[3].wait()
    wbf[y] = wfull[...].astype(BF16)
    smalls[z] = small_ref[...]
    pl.semaphore_wait(barrier, 2 * nz + 1)
    give_own(0, 0)
    give_own(1, 0)
    own_rows = held.at[z, core_rows(c), :]
    send(own_rows, own_rows, own_sem.at[0], own_sem.at[1], t, sibling)

    @pl.when(odd)
    def _():
        send(cols_ref, guest, swap.at[0], swap.at[1], other, b)

    send(wbf.at[y], wbf.at[y], w_sem.at[0], w_sem.at[1], t, across)
    near = lambda zz: jnp.logical_and(zz <= z + 1, zz >= z - 1)
    beyond = (lambda zz: zz > z + 1, lambda zz: zz < z - 1)

    def same_core(act):
        def step(zz, carry):
            @pl.when(zz != z)
            def _():
                act(zz, device(zz, y, c))

            return carry

        lax.fori_loop(0, nz, step, 0)

    same_core(lambda zz, bb: send(small_ref, smalls.at[z], small_send.at[zz], small_recv.at[z], t, bb))
    lands = (home + t) % 2

    def pass_columns(zz):
        for yy in range(2):
            ref = xblock(yy, zz, lands)
            done(ref, x_recv.at[yy, zz, lands])
            send(ref, ref, x_on.at[yy, zz], x_recv.at[yy, zz, lands], other, b)

    def take_columns():
        def step(zz, carry):
            for yy in range(2):
                done(xblock(yy, zz, 1 - lands), x_recv.at[yy, zz, 1 - lands])
            return carry

        lax.fori_loop(0, nz, step, 0)

    def half(zz, which, yy):
        return jnp.dot(held[zz, core_rows(which), :], wbf[yy], preferred_element_type=F32)

    def multiply(zz):
        for yy in range(2):
            theirs[zz, yy] = half(zz, other, yy).astype(BF16)
        send(theirs.at[zz], inbox.at[zz], pair_send.at[zz], pair_recv.at[zz], other, b)
        for yy in range(2):
            mine[zz, yy] = half(zz, t, yy)

    def give_sum(zz):
        done(inbox.at[zz], pair_recv.at[zz])
        summed[zz] = (mine[zz] + inbox[zz].astype(F32)).astype(BF16)
        bb = device(zz, y, t)
        for yy in range(2):
            slot = column(z, yy, c)
            for stays, dst, rsem in ((True, ret_ref, ret_recv), (False, layover, lay_recv)):
                right = (home == t) if stays else (home != t)

                @pl.when(jnp.logical_and(right, bb == b))
                def _():
                    pltpu.make_async_copy(summed.at[zz, yy], features(dst, slot), rsem.at[slot]).start()

                @pl.when(jnp.logical_and(right, bb != b))
                def _():
                    send(summed.at[zz, yy], features(dst, slot), sum_send.at[zz, yy], rsem.at[slot], t, bb)

    def pass_sum(zz):
        @pl.when(jnp.logical_and(c == t, zz // hz != t))
        def _():
            for yy in range(2):
                for cc in range(2):
                    j = column(zz, yy, cc)
                    done(layover.at[j], lay_recv.at[j])
                    send(layover.at[j], features(ret_ref, j), lay_send.at[j], ret_recv.at[j], other, b)

    group = 4 if nz % 4 == 0 else nz

    def product(chunk, yy):
        to = pl.ds(cuts[chunk], wide[chunk])
        total = None
        for g in range(0, nz, group):
            zs = pl.ds(g, group)
            term = lax.dot_general(
                held[zs, :, to].reshape(group * 2 * rows, wide[chunk]),
                xall[yy, zs].reshape(group * 2 * rows, cols),
                (((0,), (0,)), ((), ())),
                preferred_element_type=F32,
            )
            total = term if total is None else total + term
        return total

    def give_share(chunk):
        outputs(wsend, chunk)[...] = product(chunk, 1 - y).astype(BF16)
        send(outputs(wsend, chunk), outputs(winbox, chunk), share_send.at[chunk], share_recv.at[chunk], t, across)

    def keep_share(chunk):
        outputs(wsum_ref, chunk)[...] = product(chunk, y)

    def hop(phase, k, then):
        for chunk in phases[phase]:
            for d in range(2):
                @pl.when(k < came[d])
                def _():
                    here = piece(origin(d, k), c, chunk)
                    done(here, line_recv.at[d, k, chunk])

                    @pl.when(goes[d])
                    def _():
                        send(here, here, line_send.at[d, k + 1, chunk], line_recv.at[d, k + 1, chunk], t, ahead[d])

                    send(here, here, sib_send.at[d, k, chunk], sib_recv.at[d, k, chunk], t, sibling)

            for d in range(2):
                @pl.when(k < came[d])
                def _():
                    done(piece(origin(d, k), 1 - c, chunk), sib_recv.at[d, k, chunk])

            then(chunk)

    def gather(k, carry):
        hop(0, k, lambda chunk: None)

        @pl.when(jnp.logical_and(k == 0, odd))
        def _():
            done(guest, swap.at[1])
            give_columns(guest, near)

        @pl.when(jnp.logical_and(k == 0, jnp.logical_not(odd)))
        def _():
            give_columns(cols_ref, near)

        for d in range(2):
            @pl.when(k == jnp.maximum(came[d], min(1, last - 1)))
            def _():
                @pl.when(odd)
                def _():
                    give_columns(guest, beyond[d])

                @pl.when(jnp.logical_not(odd))
                def _():
                    give_columns(cols_ref, beyond[d])

            @pl.when(k == came[d])
            def _():
                give_own(d, 1)

        @pl.when(k == min(1, last - 1))
        def _():
            pass_columns(z)
            each(0, pass_columns)

        return carry

    lax.fori_loop(0, last, gather, 0)

    def rest(i, carry):
        each(i, pass_columns)
        return carry

    lax.fori_loop(1, last, rest, 0)
    same_core(lambda zz, bb: done(smalls.at[zz], small_recv.at[zz]))
    half_ref[...] = jnp.sum(smalls[...], axis=0)
    send(half_ref, near_ref, near_sem.at[0], near_sem.at[1], t, sibling)
    done(held.at[z, core_rows(1 - c), :], own_sem.at[1])

    done(wbf.at[1 - y], w_sem.at[1])
    multiply(z)

    def finish(k, carry):
        def then(chunk):
            if chunk < chunks - 1:
                @pl.when(k == last - 1)
                def _():
                    give_share(chunk)

        hop(1, k, then)

        each(k, multiply)

        @pl.when(k == 0)
        def _():
            take_columns()
            for chunk in early:
                give_share(chunk)

        @pl.when(k == last - 1)
        def _():
            give_share(chunks - 1)

        @pl.when(k == min(1, last - 1))
        def _():
            give_sum(z)

        @pl.when(k > 0)
        def _():
            each(k - 1, give_sum)

        @pl.when(k == 2)
        def _():
            pass_sum(z)

        @pl.when(k > 1)
        def _():
            each(k - 2, pass_sum)

        return carry

    lax.fori_loop(0, last, finish, 0)
    done(near_ref, near_sem.at[1])
    both_ref[...] = half_ref[...] + near_ref[...]
    send(both_ref, away_ref, away_sem.at[0], away_sem.at[1], t, across)
    each(last - 1, give_sum)
    for chunk in early:
        keep_share(chunk)
    if last < 3:
        pass_sum(z)
    if last > 1:
        each(last - 2, pass_sum)
    for chunk in late:
        keep_share(chunk)
    each(last - 1, pass_sum)
    keeps = []
    for chunk in range(chunks):
        done(outputs(winbox, chunk), share_recv.at[chunk])
        outputs(wsum_ref, chunk)[...] += outputs(winbox, chunk)[...].astype(F32)
        keeps.append(pltpu.make_async_copy(outputs(wsum_ref, chunk), outputs(wsum_out, chunk), out_sem.at[chunk]))
        keeps[-1].start()
    done(away_ref, away_sem.at[1])
    total_ref[...] = both_ref[...] + away_ref[...]
    for keep in keeps:
        keep.wait()

    same_core(lambda zz, bb: done(small_ref, small_send.at[zz]))
    done(half_ref, near_sem.at[0])
    done(both_ref, away_sem.at[0])
    done(own_rows, own_sem.at[0])
    done(wbf.at[y], w_sem.at[0])
    for chunk in range(chunks):
        done(outputs(wsend, chunk), share_send.at[chunk])

    @pl.when(odd)
    def _():
        done(cols_ref, swap.at[0])

    def sent_columns(j, carry):
        @pl.when(target(j) != b)
        def _():
            done(features(cols_ref, j), x_send.at[j])

        return carry

    lax.fori_loop(0, per, sent_columns, 0)

    def sent_line(zz, carry):
        for yy in range(2):
            done(xblock(yy, zz, lands), x_on.at[yy, zz])

            @pl.when(device(zz, y, t) != b)
            def _():
                done(summed.at[zz, yy], sum_send.at[zz, yy])

        done(theirs.at[zz], pair_send.at[zz])
        return carry

    lax.fori_loop(0, nz, sent_line, 0)

    def back(j, carry):
        done(features(ret_ref, j), ret_recv.at[j])

        @pl.when(c == t)
        def _():
            done(layover.at[j], lay_send.at[j])

        return carry

    lax.fori_loop(0, per, back, 0)

    def sent_pieces(k, carry):
        for chunk in range(chunks):
            for d in range(2):
                @pl.when(jnp.logical_and(goes[d], k <= came[d]))
                def _():
                    done(piece(z, c, chunk), line_send.at[d, k, chunk])

                @pl.when(k < came[d])
                def _():
                    done(piece(z, c, chunk), sib_send.at[d, k, chunk])

        return carry

    lax.fori_loop(0, last, sent_pieces, 0)


def run_exchange(nb, x_first, pre_act, cotangent, gamma, columns, weight):
    rows, outs = x_first.shape
    cols = weight.shape[1]
    nz, per = nb // 4, nb // 2
    last = nz - 1
    phases, cuts = ((0, 1), (2, 3)), tuple(outs * i // 4 for i in range(5))
    chunks = len(cuts) - 1
    dma = pltpu.SemaphoreType.DMA
    vmem = pl.BlockSpec(memory_space=pltpu.VMEM)
    far = pl.BlockSpec(memory_space=pl.ANY)
    return pl.pallas_call(
        functools.partial(exchange, nb, phases, cuts),
        out_shape=(
            jax.ShapeDtypeStruct((outs, cols), F32),
            jax.ShapeDtypeStruct(columns.shape, BF16),
            jax.ShapeDtypeStruct((2, outs), F32),
        ),
        in_specs=[far, far, far, vmem, far, far],
        out_specs=(far, far, vmem),
        scratch_shapes=[
            pltpu.VMEM((rows, outs), BF16),
            pltpu.VMEM((rows, outs), BF16),
            pltpu.VMEM((rows, outs), BF16),
            pltpu.VMEM((outs, cols), F32),
            pltpu.VMEM((nz, 2 * rows, outs), BF16),
            pltpu.VMEM((2, nz, 2 * rows, cols), BF16),
            pltpu.VMEM((nz, 2, rows, cols), F32),
            pltpu.VMEM((nz, 2, rows, cols), BF16),
            pltpu.VMEM((nz, 2, rows, cols), BF16),
            pltpu.VMEM((nz, 2, rows, cols), BF16),
            pltpu.VMEM((per, rows, cols), BF16),
            pltpu.VMEM(columns.shape, BF16),
            pltpu.VMEM((2, outs), F32),
            pltpu.VMEM((nz, 2, outs), F32),
            pltpu.VMEM((2, outs), F32),
            pltpu.VMEM((2, outs), F32),
            pltpu.VMEM((2, outs), F32),
            pltpu.VMEM((2, outs), F32),
            pltpu.VMEM((outs, cols), F32),
            pltpu.VMEM((2, outs, cols), BF16),
            pltpu.VMEM((outs, cols), BF16),
            pltpu.VMEM((outs, cols), BF16),
            dma((2, last, chunks)),
            dma((2, last, chunks)),
            dma((2, last, chunks)),
            dma((2, last, chunks)),
            dma((2,)),
            dma((2,)),
            dma((per,)),
            dma((2, nz)),
            dma((2, nz, 2)),
            dma((2,)),
            dma((nz,)),
            dma((nz,)),
            dma((nz, 2)),
            dma((per,)),
            dma((per,)),
            dma((per,)),
            dma((nz,)),
            dma((nz,)),
            dma((2,)),
            dma((2,)),
            dma((chunks,)),
            dma((chunks,)),
            dma((4,)),
            dma((chunks,)),
        ],
        compiler_params=pltpu.CompilerParams(
            collective_id=0, has_side_effects=True, vmem_limit_bytes=60 * 1024 * 1024
        ),
    )(x_first, pre_act, cotangent, gamma, columns, weight)


def results(act_ref, cot_ref, gamma_ref, share_ref, wsum_ref, total_ref, first_ref, layer_ref, weight_ref, bias_ref, sharp_ref):
    act = act_ref[...].astype(F32)
    cot = cot_ref[...].astype(F32)
    first_ref[...] = (cot * (act * jnp.tanh(gamma_ref[...] * act))).astype(BF16)
    layer_ref[...] = (cot + share_ref[...].astype(F32)).astype(BF16)
    weight_ref[...] = wsum_ref[...]
    bias_ref[...] = total_ref[0:1, :]
    sharp_ref[...] = total_ref[1:2, :]


def write_results(pre_act, cotangent, gamma, share, wsum, total):
    rows, outs = pre_act.shape
    cols = wsum.shape[1]
    steps = 2 if rows % 32 == 0 and outs % 16 == 0 else 1
    some = pl.BlockSpec((rows // steps, outs), lambda i: (i, 0))
    tile = pl.BlockSpec((outs // steps, cols), lambda i: (i, 0))
    whole = lambda n: pl.BlockSpec((n, outs), lambda i: (0, 0))
    wide = jax.ShapeDtypeStruct((rows, outs), BF16)
    flat = jax.ShapeDtypeStruct((1, outs), F32)
    return pl.pallas_call(
        results,
        grid=(steps,),
        out_shape=(wide, wide, jax.ShapeDtypeStruct((outs, cols), F32), flat, flat),
        in_specs=[some, some, whole(1), some, tile, whole(2)],
        out_specs=(some, some, tile, whole(1), whole(1)),
    )(pre_act, cotangent, gamma, share, wsum, total)


def shards(nb, x_first, x_layer, pre_act, gamma, weight, cotangent):
    rows = x_layer.shape[0]
    per, cols = nb // 2, weight.shape[1]
    aligned = cols % 128 == 0
    columns = x_layer if aligned else x_layer.reshape(rows, per, cols).transpose(1, 0, 2)
    wsum, share, total = run_exchange(nb, x_first, pre_act, cotangent, gamma[None], columns, weight)
    if not aligned:
        share = share.transpose(1, 0, 2).reshape(rows, per * cols)
    first, layer, grad_weight, bias, sharp = write_results(pre_act, cotangent, gamma[None], share, wsum, total)
    return (first, layer, grad_weight, bias[0], sharp[0])


def solution(mesh):
    assert mesh.shape["table"] == 2 and mesh.shape["batch"] % 8 == 0
    placed = (
        P("batch", "table"),
        P("batch", "table"),
        P("batch", "table"),
        P("table"),
        P("table", "batch"),
        P("batch", "table"),
    )
    return jax.shard_map(
        functools.partial(shards, mesh.shape["batch"]),
        mesh=mesh,
        in_specs=placed,
        out_specs=(
            P("batch", "table"),
            P("batch", "table"),
            P("table", "batch"),
            P("table"),
            P("table"),
        ),
        check_vma=False,
    )
```
